32 devices in a mesh: groups: 2 (over x), wide: 4 (over y, core), pair: 4 (over z).
Axes of the slice: x: 2, y: 2, z: 4, core: 2. Of those that a mesh axis runs over, the one named last changes fastest.
Arguments:
- strips: bfloat16 [8, 2, 4096, 256], P(('groups', 'wide'), None, 'pair'), parts along dimension 0, may hold values from -80 to 80
- offsets: int32 [16, 4, 2], P('groups'), parts along dimension 0, may hold values from 0 to 3328, as said below
- block_subgrid: int32 [64], P(('groups', 'wide', 'pair')), parts along dimension 0, may hold values from 0 to 1
- block_kernel: int32 [64, 2], P(('groups', 'wide', 'pair')), parts along dimension 0, may hold values from 0 to 15
- vis_cells: int32 [64, 2, 2048], P(('groups', 'wide', 'pair')), parts along dimension 0, may hold values from 0 to 248
Outputs:
- predicted: float32 [64, 2, 2048], P(('groups', 'wide', 'pair')), parts along dimension 0
The draws below stay inside these ranges and needn't reach their ends.
There are 2 independent parts, one for each index of `groups`. The reference program is written for one: setup_inputs(seed, part) draws one part's arguments, and reference() takes and returns one part's arrays. A program takes and returns all parts, laid end to end along the dimension named above; each array names one. Nothing has to cross between parts.
Inputs may be any that keep to these rules, and one draw needn't show every extreme that they name: offsets[..., 0] lies in 0 to 3328 and offsets[..., 1] in 0 to 255; both ends of both ranges occur.
All inputs are finite; a program needn't handle non-finite values.
Results may differ from the reference program's by a relative error of at most 0.0033.
The reference program's roundings to bfloat16 on the way (of `factor`, `subgrid`, `table`, `spectrum` and `row_taps`) count: a program that leaves them out, or rounds other values in their place, can miss the bound.
Values may be sent and summed in bfloat16 or wider, within the bound.
No kernel may reach another device: no remote copies, remote signals or barrier semaphores. Data moves between devices by JAX's collectives and lax.ppermute only.
A program may use at most 64 MiB of HBM per device.

```python
import math
import jax
import jax.numpy as jnp
from jax import lax

L = 4096
SUBW = 256
NVIS = 2048
SUPPORT = 8
OVERSAMPLE = 16
SG_WIDE = 2
FACETS = 4
SUBGRIDS = 8
BLK_WIDE = 8
BLOCKS = 32


def offset_plan(key):
    count = SUBGRIDS * FACETS
    row_key = jax.random.fold_in(key, 101)
    col_key = jax.random.fold_in(key, 202)
    place_key = jax.random.fold_in(key, 303)
    pick_key = jax.random.fold_in(key, 404)
    gap_key = jax.random.fold_in(key, 505)
    detune_key = jax.random.fold_in(key, 606)
    facet_ids = jnp.arange(FACETS, dtype=jnp.int32)
    row_values = jax.random.randint(row_key, (SUBGRIDS, FACETS), 0, L - 3 * SUBW + 1, dtype=jnp.int32)
    first = jax.random.randint(jax.random.fold_in(pick_key, 1), (FACETS,), 0, SUBGRIDS, dtype=jnp.int32)
    step_on = jax.random.randint(jax.random.fold_in(pick_key, 2), (FACETS,), 0, SUBGRIDS - 1, dtype=jnp.int32)
    second = (first + 1 + step_on) % SUBGRIDS
    upper_gap = jax.random.randint(jax.random.fold_in(gap_key, 1), (FACETS,), 0, SUBW, dtype=jnp.int32)
    lower_gap = jax.random.randint(jax.random.fold_in(gap_key, 2), (FACETS,), 0, SUBW, dtype=jnp.int32)
    upper_gap = upper_gap.at[0].set(0)
    lower_gap = lower_gap.at[0].set(0)
    row_values = row_values.at[first, facet_ids].set(L - 3 * SUBW - upper_gap)
    row_values = row_values.at[second, facet_ids].set(lower_gap)
    col_values = jax.random.randint(col_key, (count,), 0, SUBW, dtype=jnp.int32)
    places = jax.random.permutation(place_key, count)
    col_values = col_values.at[places[0]].set(SUBW - 1).at[places[1]].set(0)
    col_values = col_values.reshape(SUBGRIDS, FACETS)
    offsets = jnp.stack([row_values, col_values], axis=-1).astype(jnp.int32)
    detune = jax.random.randint(detune_key, (FACETS, 2), 1, SUBW // 16 + 1, dtype=jnp.int32)
    tone_up = L - 3 * SUBW - upper_gap + 3 * SUBW // 2 + detune[:, 0]
    tone_down = (lower_gap - 3 * SUBW // 2 - detune[:, 1] + L) % L
    tones = jnp.stack([tone_up, tone_down], axis=-1).astype(jnp.int32)
    return (offsets, tones)


def draw_offsets(key, part):
    offsets, tones = offset_plan(key)
    return offsets


def draw_strips(key, part):
    offsets, tones = offset_plan(key)
    noise_key = jax.random.fold_in(key, 707)
    profile_key = jax.random.fold_in(key, 808)
    noise = jnp.clip(jax.random.normal(noise_key, (FACETS, 2, L, SUBW), jnp.float32), -4.0, 4.0)
    profile = jnp.clip(jax.random.normal(profile_key, (FACETS, 2, 2, SUBW), jnp.float32), -3.0, 3.0)
    row_ids = jnp.arange(L, dtype=jnp.int32)
    turns = tones[:, :, None] * row_ids[None, None, :] % L
    phase_arg = 2.0 * math.pi / L * turns.astype(jnp.float32)
    cosine = jnp.cos(phase_arg)[..., None]
    sine = jnp.sin(phase_arg)[..., None]
    along_re = profile[:, :, 0][:, :, None, :]
    along_im = profile[:, :, 1][:, :, None, :]
    amplitude = 8.0
    tone_re = amplitude * jnp.sum(cosine * along_re - sine * along_im, axis=1)
    tone_im = amplitude * jnp.sum(sine * along_re + cosine * along_im, axis=1)
    strips = noise + jnp.stack([tone_re, tone_im], axis=1)
    return strips.astype(jnp.bfloat16)


def place_ends(array, own_key, least, high):
    index_at = [jax.random.randint(jax.random.fold_in(own_key, axis), (), 0, length) for axis, length in enumerate(array.shape)]
    main_axis = array.shape.index(max(array.shape))
    neighbour = index_at[:main_axis] + [(index_at[main_axis] + 1) % array.shape[main_axis]] + index_at[main_axis + 1:]
    return array.at[tuple(index_at)].set(least).at[tuple(neighbour)].set(high)


def setup_inputs(seed: int = 0, part: int = 0) -> dict:
    seeds = jax.random.split(jax.random.key(seed), 6)
    own_keys = jax.random.split(jax.random.fold_in(seeds[5], part), 6)
    strips = draw_strips(jax.random.fold_in(jax.random.fold_in(seeds[5], part), 71), part)
    offsets = draw_offsets(jax.random.fold_in(jax.random.fold_in(seeds[5], part), 71), part)
    block_subgrid = place_ends(jax.random.randint(own_keys[2], (BLOCKS,), 0, SG_WIDE), jax.random.fold_in(own_keys[2], 1), 0, SG_WIDE - 1).astype(jnp.int32)
    block_kernel = place_ends(jax.random.randint(own_keys[3], (BLOCKS, 2), 0, OVERSAMPLE), jax.random.fold_in(own_keys[3], 1), 0, OVERSAMPLE - 1).astype(jnp.int32)
    vis_cells = place_ends(jax.random.randint(own_keys[4], (BLOCKS, 2, NVIS), 0, SUBW - SUPPORT + 1), jax.random.fold_in(own_keys[4], 1), 0, SUBW - SUPPORT).astype(jnp.int32)
    return dict(strips=strips, offsets=offsets, block_subgrid=block_subgrid, block_kernel=block_kernel, vis_cells=vis_cells)


def strip_block(row_ids, shift, row_index, length):
    frequency = row_ids - SUBW // 2 + shift
    product = frequency[:, None] * row_index[None, :] % length
    phase_arg = 2.0 * math.pi / length * product.astype(jnp.float32)
    centred = (2 * row_index + 1).astype(jnp.float32) / length - 1.0
    taper = (1.0 - 0.5 * centred * centred) / math.sqrt(length)
    cosine = jnp.cos(phase_arg) * taper[None, :]
    sine = jnp.sin(phase_arg) * taper[None, :]
    upper = jnp.concatenate([cosine, sine], axis=1)
    lower = jnp.concatenate([-sine, cosine], axis=1)
    return jnp.concatenate([upper, lower], axis=0).astype(jnp.bfloat16)

def column_ramp(stacked, shift):
    half = stacked.shape[0] // 2
    part_re = stacked[:half]
    part_im = stacked[half:]
    column_ids = jnp.arange(SUBW, dtype=jnp.int32)
    phase_arg = 2.0 * math.pi / SUBW * (shift * column_ids % SUBW).astype(jnp.float32)
    cosine = jnp.cos(phase_arg)[None, :]
    sine = jnp.sin(phase_arg)[None, :]
    out_re = part_re * cosine + part_im * sine
    out_im = part_im * cosine - part_re * sine
    return jnp.concatenate([out_re, out_im], axis=1)

def transform_table():
    grid_ids = jnp.arange(SUBW, dtype=jnp.int32)
    phase_arg = 2.0 * math.pi / SUBW * (grid_ids[:, None] * grid_ids[None, :] % SUBW).astype(jnp.float32)
    cosine = jnp.cos(phase_arg) / math.sqrt(SUBW)
    sine = jnp.sin(phase_arg) / math.sqrt(SUBW)
    upper = jnp.concatenate([cosine, -sine], axis=1)
    lower = jnp.concatenate([sine, cosine], axis=1)
    return jnp.concatenate([upper, lower], axis=0).astype(jnp.bfloat16)

def kernel_taps(fraction):
    points = jnp.arange(SUPPORT, dtype=jnp.float32)
    centre = (SUPPORT - 1) / 2.0 + (fraction.astype(jnp.float32) + 0.5) / OVERSAMPLE - 0.5
    distance = points[None, :] - centre[:, None]
    values = jnp.exp(-distance * distance / 2.88)
    return values / lax.optimization_barrier(jnp.sum(values, axis=-1, keepdims=True))

def column_sum(spread_rows, col_ids, col_taps):
    real_part = jnp.zeros(col_ids.shape, jnp.float32)
    imag_part = jnp.zeros(col_ids.shape, jnp.float32)
    for tap_index in range(SUPPORT):
        column_at = (col_ids + tap_index)[..., None]
        weight = col_taps[..., tap_index:tap_index + 1]
        real_part = real_part + weight * jnp.take_along_axis(spread_rows, column_at, axis=-1)[..., 0]
        imag_part = imag_part + weight * jnp.take_along_axis(spread_rows, column_at + SUBW, axis=-1)[..., 0]
    return jnp.stack([real_part, imag_part], axis=-2)

def reference(strips, offsets, block_subgrid, block_kernel, vis_cells):
    xstacks = strips.reshape(FACETS, 2 * L, SUBW)
    row_index = jnp.arange(L, dtype=jnp.int32)
    all_rows = jnp.arange(SUBW, dtype=jnp.int32)
    table = transform_table()

    def single_subgrid(subgrid_id):

        def add_facet(running, facet_id):
            factor = strip_block(all_rows, offsets[subgrid_id, facet_id, 0], row_index, L)
            product = jnp.dot(factor, xstacks[facet_id], preferred_element_type=jnp.float32)
            return (running + column_ramp(product, offsets[subgrid_id, facet_id, 1]), None)
        summed, unused = lax.scan(add_facet, jnp.zeros((SUBW, 2 * SUBW), jnp.float32), jnp.arange(FACETS, dtype=jnp.int32))
        subgrid = summed.astype(jnp.bfloat16)
        return jnp.dot(subgrid, table, preferred_element_type=jnp.float32).astype(jnp.bfloat16)
    spectra = lax.map(single_subgrid, jnp.arange(SUBGRIDS, dtype=jnp.int32))
    owner = jnp.arange(BLOCKS, dtype=jnp.int32) // BLK_WIDE * SG_WIDE + block_subgrid
    row_taps = kernel_taps(block_kernel[:, 0]).astype(jnp.bfloat16)
    col_taps = kernel_taps(block_kernel[:, 1])

    def single_block(inputs):
        subgrid_id, taps_row, taps_col, cells = inputs
        spectrum = spectra[subgrid_id]
        distance = all_rows[None, :] - cells[0][:, None]
        dense = jnp.zeros((NVIS, SUBW), jnp.float32)
        for tap_index in range(SUPPORT):
            dense = jnp.where(distance == tap_index, taps_row[tap_index].astype(jnp.float32), dense)
        dense = dense.astype(jnp.bfloat16)
        spread = jnp.dot(dense, spectrum, preferred_element_type=jnp.float32)
        return column_sum(spread, cells[1], taps_col)
    return lax.map(single_block, (owner, row_taps, col_taps, vis_cells))
```

```python
import functools
import math

import jax
import jax.numpy as jnp
from jax import lax
from jax.experimental import pallas as pl
from jax.experimental.pallas import tpu as pltpu
from jax.sharding import PartitionSpec as P

L = 4096
SUBW = 256
NVIS = 2048
SUPPORT = 8
OVERSAMPLE = 16
SG_WIDE = 2
CHUNKS = 4
CW = SUBW // CHUNKS
LANES = 2 * CW
FINE = 16


def cos_sin(numerator, length):
    angle = 2.0 * math.pi / length * (numerator % length).astype(jnp.float32)
    return jnp.cos(angle), jnp.sin(angle)


def kernel_taps(fraction):
    points = jnp.arange(SUPPORT, dtype=jnp.float32)
    centre = (SUPPORT - 1) / 2.0 + (fraction.astype(jnp.float32) + 0.5) / OVERSAMPLE - 0.5
    distance = points[None, :] - centre[:, None]
    values = jnp.exp(-distance * distance / 2.88)
    return values / jnp.sum(values, axis=-1, keepdims=True)


def table_chunked():
    grid_ids = jnp.arange(SUBW, dtype=jnp.int32)
    cosine, sine = cos_sin(grid_ids[:, None] * grid_ids[None, :], SUBW)
    cosine = cosine / math.sqrt(SUBW)
    sine = sine / math.sqrt(SUBW)
    upper = jnp.concatenate([cosine, -sine], axis=1).reshape(CHUNKS, 1, CW, 2 * SUBW)
    lower = jnp.concatenate([sine, cosine], axis=1).reshape(CHUNKS, 1, CW, 2 * SUBW)
    both = jnp.concatenate([upper, lower], axis=1)
    return both.reshape(2 * SUBW, 2 * SUBW).astype(jnp.bfloat16)


def factor_kernel(turn_ref, coarse_ref, fine_ref, out_ref):
    length = turn_ref.shape[-1]
    turn_c = turn_ref[0, 0, 0:1]
    turn_s = turn_ref[0, 0, 1:2]
    fine_c = fine_ref[0]
    fine_s = fine_ref[1]
    for high in range(SUBW // FINE):
        coarse_c = coarse_ref[0, high : high + 1]
        coarse_s = coarse_ref[1, high : high + 1]
        base_c = turn_c * coarse_c - turn_s * coarse_s
        base_s = turn_s * coarse_c + turn_c * coarse_s
        rows = pl.ds(high * FINE, FINE)
        out_ref[0, 0, rows, :length] = (base_c * fine_c - base_s * fine_s).astype(jnp.bfloat16)
        out_ref[0, 0, rows, length:] = (base_s * fine_c + base_c * fine_s).astype(jnp.bfloat16)


def swap_halves(value):
    return pltpu.roll(value, CW, 1)


def ramped(factor, data, ramp_c, ramp_s):
    length = data.shape[0]
    direct = jnp.dot(factor[:, :length], data, preferred_element_type=jnp.float32)
    crossed = jnp.dot(factor[:, length:], data, preferred_element_type=jnp.float32)
    pieces = []
    for start in range(0, data.shape[1], LANES):
        lane = lax.broadcasted_iota(jnp.int32, (1, LANES), 1)
        sign = jnp.where(lane < CW, 1.0, -1.0).astype(jnp.float32)
        part = direct[:, start : start + LANES] + sign * swap_halves(
            crossed[:, start : start + LANES]
        )
        pieces.append(
            part * ramp_c[:, start : start + LANES]
            + swap_halves(part) * ramp_s[:, start : start + LANES]
        )
    return pieces


def own_kernel(factor_ref, data_ref, ramp_ref, out_ref):
    pieces = ramped(factor_ref[0, 0], data_ref[...], ramp_ref[0, 0, 0:1], ramp_ref[0, 0, 1:2])
    for index, piece in enumerate(pieces):
        out_ref[0, :, index * LANES : (index + 1) * LANES] = piece


def chunk_kernel(count, factor_ref, own_ref, ramp_ref, *refs):
    datas = refs[:count]
    keep_ref, send_ref = refs[count:]
    step = pl.program_id(0)
    total = own_ref[0]
    for index in range(count):
        total = total + ramped(
            factor_ref[index, 0], datas[index][...], ramp_ref[index, 0, 0:1], ramp_ref[index, 0, 1:2]
        )[0]
    rows = pl.ds(pl.multiple_of((step % SG_WIDE) * SUBW, SUBW), SUBW)

    @pl.when(step < SG_WIDE)
    def _():
        keep_ref[rows, :] = total

    @pl.when(step >= SG_WIDE)
    def _():
        send_ref[rows, :] = total


def degrid_kernel(pairs, pick_ref, coltap_ref, rowmat_ref, cells_ref, table_ref, *refs):
    count = CHUNKS * pairs
    pieces = refs[:count]
    out_ref, held, tall = refs[count:]
    block = pl.program_id(0)
    rows_dev = pieces[0].shape[0]

    @pl.when(block == 0)
    def _():
        place = pick_ref[1, 0]
        for chunk in range(CHUNKS):
            for step in range(pairs):
                at = pl.multiple_of((place ^ step) * rows_dev, rows_dev)
                held[pl.ds(at, rows_dev), chunk * LANES : (chunk + 1) * LANES] = pieces[
                    chunk * pairs + step
                ][...]

    first = pl.multiple_of(pick_ref[0, block] * SUBW, SUBW)
    subgrid = held[pl.ds(first, SUBW), :]
    spectrum = jnp.dot(subgrid, table_ref[...], preferred_element_type=jnp.float32).astype(
        jnp.bfloat16
    )
    tall[0 : 2 * SUBW, :] = lax.dot_general(
        spectrum, rowmat_ref[0], (((0,), (0,)), ((), ())), preferred_element_type=jnp.float32
    )
    tall[2 * SUBW :, :] = jnp.zeros((SUPPORT, SUBW), jnp.float32)
    smooth = coltap_ref[block, 0] * tall[0 : 2 * SUBW, :]
    for tap in range(1, SUPPORT):
        smooth = smooth + coltap_ref[block, tap] * tall[tap : tap + 2 * SUBW, :]
    high = smooth.astype(jnp.bfloat16)
    low = (smooth - high.astype(jnp.float32)).astype(jnp.bfloat16)
    width = 512
    for start in range(0, NVIS, width):
        row_at = cells_ref[0, 0:1, start : start + width]
        col_at = cells_ref[0, 1:2, start : start + width]
        ids = lax.broadcasted_iota(jnp.int32, (SUBW, width), 0)
        chosen = jnp.where(ids == row_at, 1.0, 0.0).astype(jnp.bfloat16)
        picked = jnp.dot(high, chosen, preferred_element_type=jnp.float32) + jnp.dot(
            low, chosen, preferred_element_type=jnp.float32
        )
        hit = ids == col_at
        out_ref[0, 0:1, start : start + width] = jnp.sum(
            jnp.where(hit, picked[:SUBW], 0.0), axis=0, keepdims=True
        )
        out_ref[0, 1:2, start : start + width] = jnp.sum(
            jnp.where(hit, picked[SUBW:], 0.0), axis=0, keepdims=True
        )


def on_device(strips, offsets, block_subgrid, block_kernel, vis_cells):
    pairs = lax.axis_size("pair")
    wides = lax.axis_size("wide")
    chips = wides // 2
    wide_id = lax.axis_index("wide")
    pair_id = lax.axis_index("pair")
    length = strips.shape[2]
    shown = 2 * SG_WIDE
    rows_dev = SG_WIDE * SUBW // pairs

    data = [
        jnp.concatenate(
            [strips[0, 0, :, i * CW : (i + 1) * CW], strips[0, 1, :, i * CW : (i + 1) * CW]], axis=1
        )
        for i in range(CHUNKS)
    ]
    arrived = [
        [
            lax.ppermute(
                part, "wide", [(w, (w + 2 * hop) % wides) for w in range(wides)]
            )
            for hop in range(1, chips)
        ]
        for part in data
    ]

    facets = (wide_id - 2 * jnp.arange(chips, dtype=jnp.int32)) % wides
    other = wide_id ^ 1
    lead = jnp.arange(SG_WIDE, dtype=jnp.int32)
    subgrids = jnp.concatenate([SG_WIDE * wide_id + lead, SG_WIDE * other + lead])
    shifts = offsets[subgrids[None, :], facets[:, None]]

    row_index = pair_id * length + jnp.arange(length, dtype=jnp.int32)
    centred = (2 * row_index + 1).astype(jnp.float32) / L - 1.0
    taper = (1.0 - 0.5 * centred * centred) / math.sqrt(L)
    turn = jnp.stack(
        cos_sin((shifts[:, :, 0] + L - SUBW // 2)[..., None] * row_index, L), axis=2
    ) * taper
    fine = jnp.stack(cos_sin(jnp.arange(FINE, dtype=jnp.int32)[:, None] * row_index, L))
    coarse = jnp.stack(
        cos_sin(jnp.arange(0, SUBW, FINE, dtype=jnp.int32)[:, None] * row_index, L)
    )
    factor = pl.pallas_call(
        factor_kernel,
        out_shape=jax.ShapeDtypeStruct((chips, shown, SUBW, 2 * length), jnp.bfloat16),
        grid=(chips, shown),
        in_specs=[
            pl.BlockSpec((1, 1, 2, length), lambda i, j: (i, j, 0, 0)),
            pl.BlockSpec((2, SUBW // FINE, length), lambda i, j: (0, 0, 0)),
            pl.BlockSpec((2, FINE, length), lambda i, j: (0, 0, 0)),
        ],
        out_specs=pl.BlockSpec((1, 1, SUBW, 2 * length), lambda i, j: (i, j, 0, 0)),
        name="factors",
    )(turn, coarse, fine)

    lanes = jnp.arange(2 * SUBW, dtype=jnp.int32)
    column = lanes // LANES * CW + lanes % CW
    ramp_c, ramp_s = cos_sin(shifts[:, :, 1][..., None] * column, SUBW)
    ramp = jnp.stack([ramp_c, jnp.where(lanes % LANES < CW, ramp_s, -ramp_s)], axis=2)

    own = pl.pallas_call(
        own_kernel,
        out_shape=jax.ShapeDtypeStruct((shown, SUBW, 2 * SUBW), jnp.float32),
        grid=(shown,),
        in_specs=[
            pl.BlockSpec((1, 1, SUBW, 2 * length), lambda j: (0, j, 0, 0)),
            pl.BlockSpec((length, 2 * SUBW), lambda j: (0, 0)),
            pl.BlockSpec((1, 1, 2, 2 * SUBW), lambda j: (0, j, 0, 0)),
        ],
        out_specs=pl.BlockSpec((1, SUBW, 2 * SUBW), lambda j: (j, 0, 0)),
        name="own_facet",
    )(factor, jnp.concatenate(data, axis=1), ramp)

    factor_rest = factor[1:]
    ramp_rest = ramp[1:]

    def chunk_sums(index):
        hops = chips - 1
        return pl.pallas_call(
            functools.partial(chunk_kernel, hops),
            out_shape=[jax.ShapeDtypeStruct((SG_WIDE * SUBW, LANES), jnp.float32)] * 2,
            grid=(shown,),
            in_specs=[
                pl.BlockSpec((hops, 1, SUBW, 2 * length), lambda j: (0, j, 0, 0)),
                pl.BlockSpec((1, SUBW, LANES), lambda j: (j, 0, index)),
                pl.BlockSpec((hops, 1, 2, LANES), lambda j: (0, j, 0, index)),
            ]
            + [pl.BlockSpec((length, LANES), lambda j: (0, 0))] * hops,
            out_specs=[pl.BlockSpec((SG_WIDE * SUBW, LANES), lambda j: (0, 0))] * 2,
            name="chunk_sums",
        )(factor_rest, own, ramp_rest, *arrived[index])

    def reduce_rows(index):
        keep, send = chunk_sums(index)
        total = keep + lax.ppermute(send, "wide", [(w, w ^ 1) for w in range(wides)])
        bits = pairs.bit_length() - 1
        total = total.reshape((2,) * bits + (rows_dev, LANES))
        for bit in range(bits):
            axis = total.ndim - 3
            mine = (pair_id >> bit) & 1
            passed = lax.dynamic_index_in_dim(total, 1 - mine, axis, keepdims=False)
            held = lax.dynamic_index_in_dim(total, mine, axis, keepdims=False)
            total = held + lax.ppermute(
                passed, "pair", [(p, p ^ (1 << bit)) for p in range(pairs)]
            )
        rounded = total.astype(jnp.bfloat16)
        return [rounded] + [
            lax.ppermute(rounded, "pair", [(p, p ^ step) for p in range(pairs)])
            for step in range(1, pairs)
        ]

    pieces = [piece for index in range(CHUNKS) for piece in reduce_rows(index)]

    blocks = vis_cells.shape[0]
    row_taps = kernel_taps(block_kernel[:, 0]).astype(jnp.bfloat16)
    col_taps = kernel_taps(block_kernel[:, 1])
    ids = jnp.arange(SUBW, dtype=jnp.int32)
    distance = ids[:, None] - ids[None, :]
    row_matrix = jnp.zeros((blocks, SUBW, SUBW), jnp.float32)
    for tap in range(SUPPORT):
        row_matrix = jnp.where(
            distance == tap, row_taps[:, tap].astype(jnp.float32)[:, None, None], row_matrix
        )
    row_matrix = row_matrix.astype(jnp.bfloat16)
    picks = jnp.stack([block_subgrid, jnp.full_like(block_subgrid, pair_id)])

    return pl.pallas_call(
        functools.partial(degrid_kernel, pairs),
        out_shape=jax.ShapeDtypeStruct((blocks, 2, NVIS), jnp.float32),
        grid=(blocks,),
        in_specs=[
            pl.BlockSpec(memory_space=pltpu.SMEM),
            pl.BlockSpec(memory_space=pltpu.SMEM),
            pl.BlockSpec((1, SUBW, SUBW), lambda b: (b, 0, 0)),
            pl.BlockSpec((1, 2, NVIS), lambda b: (b, 0, 0)),
            pl.BlockSpec((2 * SUBW, 2 * SUBW), lambda b: (0, 0)),
        ]
        + [pl.BlockSpec((rows_dev, LANES), lambda b: (0, 0))] * len(pieces),
        out_specs=pl.BlockSpec((1, 2, NVIS), lambda b: (b, 0, 0)),
        scratch_shapes=[
            pltpu.VMEM((SG_WIDE * SUBW, 2 * SUBW), jnp.bfloat16),
            pltpu.VMEM((2 * SUBW + SUPPORT, SUBW), jnp.float32),
        ],
        name="degrid",
    )(picks, col_taps, row_matrix, vis_cells, table_chunked(), *pieces)


def solution(mesh):
    placed = (
        P(("groups", "wide"), None, "pair", None),
        P("groups", None, None),
        P(("groups", "wide", "pair")),
        P(("groups", "wide", "pair"), None),
        P(("groups", "wide", "pair"), None, None),
    )
    return jax.shard_map(
        on_device,
        mesh=mesh,
        in_specs=placed,
        out_specs=P(("groups", "wide", "pair"), None, None),
        check_vma=False,
    )
```

```python
import functools
import math

import jax
import jax.numpy as jnp
import ml_dtypes
import numpy as np
from jax import lax
from jax.experimental import pallas as pl
from jax.experimental.pallas import tpu as pltpu
from jax.sharding import PartitionSpec as P

L = 4096
SUBW = 256
NVIS = 2048
SUPPORT = 8
OVERSAMPLE = 16
SG_WIDE = 2
SHOWN = 2 * SG_WIDE
CHUNKS = 2
CW = SUBW // CHUNKS
LANES = 2 * CW
FINE = 16
VMEM_LIMIT = 56 << 20

TURN = float(np.float32(2.0 * math.pi / L))
TURN_HIGH = float(np.float32(np.round(2.0 * math.pi / L * 2**20) / 2**20))
TURN_LOW = 2.0 * math.pi / L - TURN_HIGH


def kernel_taps(fraction):
    points = jnp.arange(SUPPORT, dtype=jnp.float32)
    centre = (SUPPORT - 1) / 2.0 + (fraction.astype(jnp.float32) + 0.5) / OVERSAMPLE - 0.5
    distance = points[None, :] - centre[:, None]
    values = jnp.exp(-distance * distance / 2.88)
    return values / jnp.sum(values, axis=-1, keepdims=True)


def table_chunked():
    grid_ids = np.arange(SUBW)
    phase = 2.0 * math.pi / SUBW * (grid_ids[:, None] * grid_ids[None, :] % SUBW)
    cosine = np.cos(phase) / math.sqrt(SUBW)
    sine = np.sin(phase) / math.sqrt(SUBW)
    upper = np.concatenate([cosine, -sine], axis=1).reshape(CHUNKS, 1, CW, 2 * SUBW)
    lower = np.concatenate([sine, cosine], axis=1).reshape(CHUNKS, 1, CW, 2 * SUBW)
    both = np.concatenate([upper, lower], axis=1).reshape(2 * SUBW, 2 * SUBW)
    return jnp.asarray(both.astype(np.float32).astype(ml_dtypes.bfloat16))


def cos_sin(number):
    quarter = lax.shift_right_logical(number + L // 8, int(math.log2(L // 4)))
    angle = (number - quarter * (L // 4)).astype(jnp.float32) * TURN
    square = angle * angle
    sine = 1.0 / 362880
    for term in (-1.0 / 5040, 1.0 / 120, -1.0 / 6, 1.0):
        sine = sine * square + term
    sine = sine * angle
    cosine = -1.0 / 3628800
    for term in (1.0 / 40320, -1.0 / 720, 1.0 / 24, -0.5, 1.0):
        cosine = cosine * square + term
    odd = (quarter & 1) == 1
    first = jnp.where(odd, sine, cosine)
    second = jnp.where(odd, cosine, sine)
    first = jnp.where(((quarter + 1) & 2) == 2, -first, first)
    second = jnp.where((quarter & 2) == 2, -second, second)
    return first, second


def ramp_of(shift):
    lane = lax.broadcasted_iota(jnp.int32, (1, 2 * SUBW), 1)
    column = lane // LANES * CW + lane % CW
    cosine, sine = cos_sin((shift * column) % SUBW * (L // SUBW))
    return cosine, jnp.where(lane % LANES < CW, sine, -sine)


def swap_halves(value):
    return jnp.concatenate([value[:, CW:], value[:, :CW]], axis=1)


def ramped(direct, crossed, cosine, sine):
    part = direct + jnp.concatenate([crossed[:, CW:], -crossed[:, :CW]], axis=1)
    return part * cosine + swap_halves(part) * sine


def prep_kernel(chips, shift_ref, place_ref, strips_ref, rest_ref, own_ref, fine, fine_at, base, base_at, held):
    length = strips_ref.shape[1]
    row_ids = place_ref[0] + lax.broadcasted_iota(jnp.int32, (FINE, length), 1)
    group = lax.broadcasted_iota(jnp.int32, (FINE, length), 0)
    centred = (2 * row_ids + 1).astype(jnp.float32) / L - 1.0
    taper = (1.0 - 0.5 * centred * centred) / math.sqrt(L)
    number = (group * row_ids) & (L - 1)
    fine_at[...] = number
    cosine, sine = cos_sin(number)
    fine[0] = cosine
    fine[1] = sine

    def make_factor(facet, shown, store):
        shift = shift_ref[facet, shown, 0] + (L - SUBW // 2)
        number = ((shift + FINE * group) * row_ids) & (L - 1)
        base_at[...] = number
        cosine, sine = cos_sin(number)
        base[0] = cosine * taper
        base[1] = sine * taper

        def one_group(high, carry):
            at = (base_at[pl.ds(high, 1), :] + fine_at[...]) & (L - 1)
            count = at.astype(jnp.float32)
            turned = count * TURN
            slip = (turned - count * TURN_HIGH) - count * TURN_LOW
            base_c = base[0, pl.ds(high, 1), :]
            base_s = base[1, pl.ds(high, 1), :]
            cosine = base_c * fine[0] - base_s * fine[1]
            sine = base_s * fine[0] + base_c * fine[1]
            rows = pl.ds(pl.multiple_of(high * FINE, FINE), FINE)
            store(
                rows,
                (cosine - slip * sine).astype(jnp.bfloat16),
                (sine + slip * cosine).astype(jnp.bfloat16),
            )
            return carry

        lax.fori_loop(0, SUBW // FINE, one_group, 0, unroll=2)

    def own_step(shown, carry):
        def store(rows, cosine, sine):
            held[rows, :length] = cosine
            held[rows, length:] = sine

        make_factor(0, shown, store)
        ramp_c, ramp_s = ramp_of(shift_ref[0, shown, 1])
        for chunk in range(CHUNKS):
            columns = slice(chunk * CW, (chunk + 1) * CW)
            lanes = slice(chunk * LANES, (chunk + 1) * LANES)
            data = jnp.concatenate([strips_ref[0, :, columns], strips_ref[1, :, columns]], axis=1)
            direct = jnp.dot(held[:, :length], data, preferred_element_type=jnp.float32)
            crossed = jnp.dot(held[:, length:], data, preferred_element_type=jnp.float32)
            own_ref[chunk, shown] = ramped(direct, crossed, ramp_c[:, lanes], ramp_s[:, lanes])
        return carry

    lax.fori_loop(0, SHOWN, own_step, 0)

    def rest_step(step, carry):
        facet = step // SHOWN
        shown = step % SHOWN

        def store(rows, cosine, sine):
            rest_ref[facet, shown, rows, :length] = cosine
            rest_ref[facet, shown, rows, length:] = sine

        make_factor(facet + 1, shown, store)
        return carry

    lax.fori_loop(0, (chips - 1) * SHOWN, rest_step, 0)


def chunk_kernel(chunk, shift_ref, rest_ref, own_ref, *refs):
    hops = len(refs) - 2
    keep_ref, send_ref = refs[hops:]
    lanes = slice(chunk * LANES, (chunk + 1) * LANES)
    length = refs[0].shape[1]
    for shown in range(SHOWN):
        total = own_ref[chunk, shown]
        for hop in range(hops):
            data = jnp.concatenate([refs[hop][0], refs[hop][1]], axis=1)
            ramp_c, ramp_s = ramp_of(shift_ref[hop + 1, shown, 1])
            direct = jnp.dot(
                rest_ref[hop, shown, :, :length], data, preferred_element_type=jnp.float32
            )
            crossed = jnp.dot(
                rest_ref[hop, shown, :, length:], data, preferred_element_type=jnp.float32
            )
            total = total + ramped(direct, crossed, ramp_c[:, lanes], ramp_s[:, lanes])
        target = keep_ref if shown < SG_WIDE else send_ref
        first = shown % SG_WIDE * SUBW
        target[first : first + SUBW, :] = total


def degrid_kernel(pairs, pick_ref, rowtap_ref, coltap_ref, cells_ref, table_ref, *refs):
    count = CHUNKS * pairs
    pieces = refs[:count]
    out_ref, held, tall = refs[count:]
    blocks = cells_ref.shape[0]
    rows_dev = pieces[0].shape[0]
    place = pick_ref[1, 0]
    for chunk in range(CHUNKS):
        for step in range(pairs):
            at = pl.multiple_of((place ^ step) * rows_dev, rows_dev)
            held[pl.ds(at, rows_dev), chunk * LANES : (chunk + 1) * LANES] = pieces[
                chunk * pairs + step
            ][...]
    tall[2 * SUBW :, :] = jnp.zeros((SUPPORT, SUBW), jnp.float32)
    ids = lax.broadcasted_iota(jnp.int32, (SUBW, SUBW), 0)
    distance = ids - lax.broadcasted_iota(jnp.int32, (SUBW, SUBW), 1)
    width = 512

    for block in range(blocks):
        row_matrix = jnp.zeros((SUBW, SUBW), jnp.float32)
        for tap in range(SUPPORT):
            row_matrix = jnp.where(distance == tap, rowtap_ref[block, tap], row_matrix)
        first = pl.multiple_of(pick_ref[0, block] * SUBW, SUBW)
        subgrid = held[pl.ds(first, SUBW), :]
        spectrum = jnp.dot(subgrid, table_ref[...], preferred_element_type=jnp.float32).astype(
            jnp.bfloat16
        )
        tall[0 : 2 * SUBW, :] = lax.dot_general(
            spectrum,
            row_matrix.astype(jnp.bfloat16),
            (((0,), (0,)), ((), ())),
            preferred_element_type=jnp.float32,
        )
        smooth = coltap_ref[block, 0] * tall[0 : 2 * SUBW, :]
        for tap in range(1, SUPPORT):
            smooth = smooth + coltap_ref[block, tap] * tall[tap : tap + 2 * SUBW, :]
        high = smooth.astype(jnp.bfloat16)
        low = (smooth - high.astype(jnp.float32)).astype(jnp.bfloat16)
        for start in range(0, NVIS, width):
            row_at = cells_ref[block, 0:1, start : start + width]
            col_at = cells_ref[block, 1:2, start : start + width]
            wide_ids = lax.broadcasted_iota(jnp.int32, (SUBW, width), 0)
            chosen = jnp.where(wide_ids == row_at, 1.0, 0.0).astype(jnp.bfloat16)
            picked = jnp.dot(high, chosen, preferred_element_type=jnp.float32) + jnp.dot(
                low, chosen, preferred_element_type=jnp.float32
            )
            hit = wide_ids == col_at
            out_ref[block, 0:1, start : start + width] = jnp.sum(
                jnp.where(hit, picked[:SUBW], 0.0), axis=0, keepdims=True
            )
            out_ref[block, 1:2, start : start + width] = jnp.sum(
                jnp.where(hit, picked[SUBW:], 0.0), axis=0, keepdims=True
            )


def on_device(strips, offsets, block_subgrid, block_kernel, vis_cells):
    pairs = lax.axis_size("pair")
    wides = lax.axis_size("wide")
    chips = wides // 2
    wide_id = lax.axis_index("wide")
    pair_id = lax.axis_index("pair")
    length = strips.shape[2]
    rows_dev = SG_WIDE * SUBW // pairs
    in_smem = pl.BlockSpec(memory_space=pltpu.SMEM)
    in_vmem = pl.BlockSpec(memory_space=pltpu.VMEM)
    params = pltpu.CompilerParams(vmem_limit_bytes=VMEM_LIMIT)

    strips = strips[0]
    arrived = [
        [
            lax.ppermute(
                strips[:, :, i * CW : (i + 1) * CW],
                "wide",
                [(w, (w + 2 * hop) % wides) for w in range(wides)],
            )
            for hop in range(1, chips)
        ]
        for i in range(CHUNKS)
    ]

    facets = (wide_id - 2 * jnp.arange(chips, dtype=jnp.int32)) % wides
    lead = jnp.arange(SG_WIDE, dtype=jnp.int32)
    subgrids = jnp.concatenate([SG_WIDE * wide_id + lead, SG_WIDE * (wide_id ^ 1) + lead])
    shifts = offsets[subgrids[None, :], facets[:, None]]
    place = (pair_id * length).reshape(1)

    rest, own = pl.pallas_call(
        functools.partial(prep_kernel, chips),
        out_shape=[
            jax.ShapeDtypeStruct((chips - 1, SHOWN, SUBW, 2 * length), jnp.bfloat16),
            jax.ShapeDtypeStruct((CHUNKS, SHOWN, SUBW, LANES), jnp.float32),
        ],
        in_specs=[in_smem, in_smem, in_vmem],
        out_specs=[in_vmem, in_vmem],
        scratch_shapes=[
            pltpu.VMEM((2, FINE, length), jnp.float32),
            pltpu.VMEM((FINE, length), jnp.int32),
            pltpu.VMEM((2, FINE, length), jnp.float32),
            pltpu.VMEM((FINE, length), jnp.int32),
            pltpu.VMEM((SUBW, 2 * length), jnp.bfloat16),
        ],
        compiler_params=params,
        name="prepare",
    )(shifts, place, strips)

    def chunk_sums(index):
        return pl.pallas_call(
            functools.partial(chunk_kernel, index),
            out_shape=[jax.ShapeDtypeStruct((SG_WIDE * SUBW, LANES), jnp.float32)] * 2,
            in_specs=[in_smem, in_vmem, in_vmem] + [in_vmem] * (chips - 1),
            out_specs=[in_vmem] * 2,
            compiler_params=params,
            name="chunk_sums",
        )(shifts, rest, own, *arrived[index])

    def reduce_rows(index):
        keep, send = chunk_sums(index)
        total = keep + lax.ppermute(send, "wide", [(w, w ^ 1) for w in range(wides)])
        bits = pairs.bit_length() - 1
        total = total.reshape((2,) * bits + (rows_dev, LANES))
        for bit in range(bits):
            axis = total.ndim - 3
            mine = (pair_id >> bit) & 1
            passed = lax.dynamic_index_in_dim(total, 1 - mine, axis, keepdims=False)
            held = lax.dynamic_index_in_dim(total, mine, axis, keepdims=False)
            total = held + lax.ppermute(
                passed, "pair", [(p, p ^ (1 << bit)) for p in range(pairs)]
            )
        rounded = total.astype(jnp.bfloat16)
        return [rounded] + [
            lax.ppermute(rounded, "pair", [(p, p ^ step) for p in range(pairs)])
            for step in range(1, pairs)
        ]

    pieces = [piece for index in range(CHUNKS) for piece in reduce_rows(index)]

    blocks = vis_cells.shape[0]
    row_taps = kernel_taps(block_kernel[:, 0]).astype(jnp.bfloat16).astype(jnp.float32)
    col_taps = kernel_taps(block_kernel[:, 1])
    picks = jnp.stack([block_subgrid, jnp.full_like(block_subgrid, pair_id)])

    return pl.pallas_call(
        functools.partial(degrid_kernel, pairs),
        out_shape=jax.ShapeDtypeStruct((blocks, 2, NVIS), jnp.float32),
        in_specs=[in_smem] * 3 + [in_vmem] * (2 + len(pieces)),
        out_specs=in_vmem,
        scratch_shapes=[
            pltpu.VMEM((SG_WIDE * SUBW, 2 * SUBW), jnp.bfloat16),
            pltpu.VMEM((2 * SUBW + SUPPORT, SUBW), jnp.float32),
        ],
        compiler_params=params,
        name="degrid",
    )(picks, row_taps, col_taps, vis_cells, table_chunked(), *pieces)


def solution(mesh):
    placed = (
        P(("groups", "wide"), None, "pair", None),
        P("groups", None, None),
        P(("groups", "wide", "pair")),
        P(("groups", "wide", "pair"), None),
        P(("groups", "wide", "pair"), None, None),
    )
    return jax.shard_map(
        on_device,
        mesh=mesh,
        in_specs=placed,
        out_specs=P(("groups", "wide", "pair"), None, None),
        check_vma=False,
    )
```

```python
import functools
import math

import jax
import jax.numpy as jnp
import ml_dtypes
import numpy as np
from jax import lax
from jax.experimental import pallas as pl
from jax.experimental.pallas import tpu as pltpu
from jax.sharding import PartitionSpec as P

L = 4096
SUBW = 256
NVIS = 2048
SUPPORT = 8
OVERSAMPLE = 16
SG_WIDE = 2
SHOWN = 2 * SG_WIDE
CHUNKS = 2
CW = SUBW // CHUNKS
LANES = 2 * CW
FINE = 16
VMEM_LIMIT = 20 << 20

TURN = float(np.float32(2.0 * math.pi / L))
TURN_HIGH = float(np.float32(np.round(2.0 * math.pi / L * 2**20) / 2**20))
TURN_LOW = 2.0 * math.pi / L - TURN_HIGH


def tap_shape(fraction):
    centre = (SUPPORT - 1) / 2.0 + (fraction.astype(jnp.float32) + 0.5) / OVERSAMPLE - 0.5
    point = lax.broadcasted_iota(jnp.int32, (SUPPORT, 128), 0).astype(jnp.float32)
    distance = point - centre
    total = jnp.sum(jnp.exp(-distance * distance / 2.88), axis=0, keepdims=True)
    return centre, -jnp.log2(total)[:, 0:1]


def table_chunked():
    grid_ids = np.arange(SUBW)
    phase = 2.0 * math.pi / SUBW * (grid_ids[:, None] * grid_ids[None, :] % SUBW)
    cosine = np.cos(phase) / math.sqrt(SUBW)
    sine = np.sin(phase) / math.sqrt(SUBW)
    upper = np.concatenate([cosine, -sine], axis=1).reshape(CHUNKS, 1, CW, 2 * SUBW)
    lower = np.concatenate([sine, cosine], axis=1).reshape(CHUNKS, 1, CW, 2 * SUBW)
    both = np.concatenate([upper, lower], axis=1).reshape(2 * SUBW, 2 * SUBW)
    return jnp.asarray(both.T.astype(np.float32).astype(ml_dtypes.bfloat16))


def cos_sin(number):
    quarter = lax.shift_right_logical(number + L // 8, int(math.log2(L // 4)))
    angle = (number - quarter * (L // 4)).astype(jnp.float32) * TURN
    square = angle * angle
    sine = 1.0 / 362880
    for term in (-1.0 / 5040, 1.0 / 120, -1.0 / 6, 1.0):
        sine = sine * square + term
    sine = sine * angle
    cosine = -1.0 / 3628800
    for term in (1.0 / 40320, -1.0 / 720, 1.0 / 24, -0.5, 1.0):
        cosine = cosine * square + term
    odd = (quarter & 1) == 1
    first = jnp.where(odd, sine, cosine)
    second = jnp.where(odd, cosine, sine)
    first = jnp.where(((quarter + 1) & 2) == 2, -first, first)
    second = jnp.where((quarter & 2) == 2, -second, second)
    return first, second


def ramp_of(shift):
    lane = lax.broadcasted_iota(jnp.int32, (1, 2 * SUBW), 1)
    column = lane // LANES * CW + lane % CW
    cosine, sine = cos_sin((shift * column) % SUBW * (L // SUBW))
    return cosine, jnp.where(lane % LANES < CW, sine, -sine)


def cost(flops):
    return pl.CostEstimate(flops=flops, bytes_accessed=1 << 20, transcendentals=0)


def swap_halves(value):
    return jnp.concatenate([value[:, CW:], value[:, :CW]], axis=1)


def ramped(direct, crossed, cosine, sine):
    part = direct + jnp.concatenate([crossed[:, CW:], -crossed[:, :CW]], axis=1)
    return part * cosine + swap_halves(part) * sine


def shift_of(offset_ref, place_ref, wides, hop, shown, part):
    wide_id = place_ref[1]
    owner = wide_id ^ (shown // SG_WIDE)
    facet = lax.rem(wide_id - 2 * hop + wides, wides)
    return offset_ref[SG_WIDE * owner + shown % SG_WIDE, facet, part]


def prep_kernel(wides, offset_ref, place_ref, strips_hbm, rest_ref, own_ref, fine, fine_at, base, base_at, held, strips_ref, arrival):
    chips = wides // 2
    shift_at = functools.partial(shift_of, offset_ref, place_ref, wides)
    length = strips_ref.shape[1]
    copy = pltpu.make_async_copy(strips_hbm, strips_ref, arrival)
    copy.start()
    row_ids = place_ref[0] + lax.broadcasted_iota(jnp.int32, (FINE, length), 1)
    group = lax.broadcasted_iota(jnp.int32, (FINE, length), 0)
    centred = (2 * row_ids + 1).astype(jnp.float32) / L - 1.0
    taper = (1.0 - 0.5 * centred * centred) / math.sqrt(L)
    number = (group * row_ids) & (L - 1)
    fine_at[...] = number
    cosine, sine = cos_sin(number)
    fine[0] = cosine
    fine[1] = sine

    def make_factor(facet, shown, store):
        shift = shift_at(facet, shown, 0) + (L - SUBW // 2)
        number = ((shift + FINE * group) * row_ids) & (L - 1)
        base_at[...] = number
        cosine, sine = cos_sin(number)
        base[0] = cosine * taper
        base[1] = sine * taper

        def one_group(high, carry):
            at = (base_at[pl.ds(high, 1), :] + fine_at[...]) & (L - 1)
            count = at.astype(jnp.float32)
            turned = count * TURN
            slip = (turned - count * TURN_HIGH) - count * TURN_LOW
            base_c = base[0, pl.ds(high, 1), :]
            base_s = base[1, pl.ds(high, 1), :]
            cosine = base_c * fine[0] - base_s * fine[1]
            sine = base_s * fine[0] + base_c * fine[1]
            rows = pl.ds(pl.multiple_of(high * FINE, FINE), FINE)
            store(
                rows,
                (cosine - slip * sine).astype(jnp.bfloat16),
                (sine + slip * cosine).astype(jnp.bfloat16),
            )
            return carry

        lax.fori_loop(0, SUBW // FINE, one_group, 0, unroll=2)

    def rest_step(step, carry):
        facet = step // SHOWN
        shown = step % SHOWN

        def store(rows, cosine, sine):
            rest_ref[facet, shown, rows, :length] = cosine
            rest_ref[facet, shown, rows, length:] = sine

        make_factor(facet + 1, shown, store)
        return carry

    lax.fori_loop(0, (chips - 1) * SHOWN, rest_step, 0)
    copy.wait()

    def own_step(shown, carry):
        def store(rows, cosine, sine):
            held[rows, :length] = cosine
            held[rows, length:] = sine

        make_factor(0, shown, store)
        ramp_c, ramp_s = ramp_of(shift_at(0, shown, 1))
        for chunk in range(CHUNKS):
            columns = slice(chunk * CW, (chunk + 1) * CW)
            lanes = slice(chunk * LANES, (chunk + 1) * LANES)
            data = jnp.concatenate([strips_ref[0, :, columns], strips_ref[1, :, columns]], axis=1)
            direct = jnp.dot(held[:, :length], data, preferred_element_type=jnp.float32)
            crossed = jnp.dot(held[:, length:], data, preferred_element_type=jnp.float32)
            own_ref[chunk, shown] = ramped(direct, crossed, ramp_c[:, lanes], ramp_s[:, lanes])
        return carry

    lax.fori_loop(0, SHOWN, own_step, 0)


def chunk_kernel(chunk, wides, offset_ref, place_ref, rest_ref, own_ref, *refs):
    hops = wides // 2 - 1
    keep_ref, send_ref = refs[-2:]
    lanes = slice(chunk * LANES, (chunk + 1) * LANES)
    length = refs[0].shape[1]
    for shown in range(SHOWN):
        total = own_ref[chunk, shown]
        for hop in range(hops):
            data = jnp.concatenate([refs[hop][0], refs[hop][1]], axis=1)
            ramp_c, ramp_s = ramp_of(shift_of(offset_ref, place_ref, wides, hop + 1, shown, 1))
            direct = jnp.dot(
                rest_ref[hop, shown, :, :length], data, preferred_element_type=jnp.float32
            )
            crossed = jnp.dot(
                rest_ref[hop, shown, :, length:], data, preferred_element_type=jnp.float32
            )
            total = total + ramped(direct, crossed, ramp_c[:, lanes], ramp_s[:, lanes])
        target = keep_ref if shown < SG_WIDE else send_ref
        first = shown % SG_WIDE * SUBW
        target[first : first + SUBW, :] = total


def weight_kernel(fraction_ref, cells_ref, row_ref, col_ref):
    width = 512
    scale = -1.0 / (2.88 * math.log(2.0))
    ids = lax.broadcasted_iota(jnp.int32, (SUBW, width), 0).astype(jnp.float32)
    for block in range(cells_ref.shape[0]):
        for part, target in ((0, row_ref), (1, col_ref)):
            centre, norm = tap_shape(fraction_ref[block, part])

            def one_part(step, carry):
                lanes = pl.ds(pl.multiple_of(step * width, width), width)
                distance = ids - cells_ref[block, part : part + 1, lanes].astype(jnp.float32)
                offset = distance - centre
                values = jnp.exp2(offset * offset * scale + norm)
                inside = jnp.abs(distance - (SUPPORT - 1) / 2.0) < SUPPORT / 2.0
                target[block, :, lanes] = jnp.where(inside, values, 0.0).astype(target.dtype)
                return carry

            lax.fori_loop(0, NVIS // width, one_part, 0)


def degrid_kernel(pairs, place_ref, pick_ref, row_ref, col_ref, table_ref, *refs):
    count = CHUNKS * pairs
    pieces = refs[:count]
    out_ref, held = refs[count:]
    rows_dev = pieces[0].shape[0]
    place = place_ref[2]
    for chunk in range(CHUNKS):
        for step in range(pairs):
            at = pl.multiple_of((place ^ step) * rows_dev, rows_dev)
            held[pl.ds(at, rows_dev), chunk * LANES : (chunk + 1) * LANES] = pieces[
                chunk * pairs + step
            ][...]
    width = 512
    for block in range(row_ref.shape[0]):
        first = pl.multiple_of(pick_ref[block] * SUBW, SUBW)
        spectrum = lax.dot_general(
            table_ref[...],
            held[pl.ds(first, SUBW), :],
            (((1,), (1,)), ((), ())),
            preferred_element_type=jnp.float32,
        ).astype(jnp.bfloat16)
        for start in range(0, NVIS, width):
            lanes = slice(start, start + width)
            spread = jnp.dot(
                spectrum, row_ref[block, :, lanes], preferred_element_type=jnp.float32
            )
            weights = col_ref[block, :, lanes]
            out_ref[block, 0:1, lanes] = jnp.sum(weights * spread[:SUBW], axis=0, keepdims=True)
            out_ref[block, 1:2, lanes] = jnp.sum(weights * spread[SUBW:], axis=0, keepdims=True)


def on_device(strips, offsets, block_subgrid, block_kernel, vis_cells):
    pairs = lax.axis_size("pair")
    wides = lax.axis_size("wide")
    chips = wides // 2
    wide_id = lax.axis_index("wide")
    pair_id = lax.axis_index("pair")
    length = strips.shape[2]
    rows_dev = SG_WIDE * SUBW // pairs
    in_smem = pl.BlockSpec(memory_space=pltpu.SMEM)
    in_vmem = pl.BlockSpec(memory_space=pltpu.VMEM)
    anywhere = pl.BlockSpec(memory_space=pl.ANY)
    params = pltpu.CompilerParams(vmem_limit_bytes=VMEM_LIMIT)

    strips = strips[0]
    arrived = []
    whole = strips
    for index in range(CHUNKS):
        part = whole[:, :, index * CW : (index + 1) * CW]
        whole, part = lax.optimization_barrier((whole, part))
        arrived.append(
            [
                lax.ppermute(part, "wide", [(w, (w + 2 * hop) % wides) for w in range(wides)])
                for hop in range(1, chips)
            ]
        )

    place = jnp.stack([pair_id * length, wide_id, pair_id])

    rest, own = pl.pallas_call(
        functools.partial(prep_kernel, wides),
        out_shape=[
            jax.ShapeDtypeStruct((chips - 1, SHOWN, SUBW, 2 * length), jnp.bfloat16),
            jax.ShapeDtypeStruct((CHUNKS, SHOWN, SUBW, LANES), jnp.float32),
        ],
        in_specs=[in_smem, in_smem, anywhere],
        out_specs=[in_vmem, in_vmem],
        scratch_shapes=[
            pltpu.VMEM((2, FINE, length), jnp.float32),
            pltpu.VMEM((FINE, length), jnp.int32),
            pltpu.VMEM((2, FINE, length), jnp.float32),
            pltpu.VMEM((FINE, length), jnp.int32),
            pltpu.VMEM((SUBW, 2 * length), jnp.bfloat16),
            pltpu.VMEM((2, length, SUBW), jnp.bfloat16),
            pltpu.SemaphoreType.DMA,
        ],
        compiler_params=params,
        cost_estimate=cost(12100000000),
        name="prepare",
    )(offsets, place, strips)

    bits = pairs.bit_length() - 1

    def start_chunk(index):
        keep, send = pl.pallas_call(
            functools.partial(chunk_kernel, index, wides),
            out_shape=[jax.ShapeDtypeStruct((SG_WIDE * SUBW, LANES), jnp.float32)] * 2,
            in_specs=[in_smem, in_smem] + [in_vmem] * (chips + 1),
            out_specs=[in_vmem] * 2,
            compiler_params=params,
            cost_estimate=cost(2420000000),
        name="chunk_sums",
        )(offsets, place, rest, own, *arrived[index])
        other = lax.ppermute(send, "wide", [(w, w ^ 1) for w in range(wides)])
        shape = (2,) * bits + (rows_dev, LANES)
        return halved(keep.reshape(shape), other.reshape(shape), 0)

    def halved(first, second, bit):
        axis = first.ndim - 3
        mine = (pair_id >> bit) & 1
        passed, held = [
            lax.dynamic_index_in_dim(first, side, axis, keepdims=False)
            + lax.dynamic_index_in_dim(second, side, axis, keepdims=False)
            for side in (1 - mine, mine)
        ]
        return passed, held

    def exchange(passed, bit):
        return lax.ppermute(passed, "pair", [(p, p ^ (1 << bit)) for p in range(pairs)])

    blocks = vis_cells.shape[0]
    halves = []
    for index in range(CHUNKS):
        passed, held = start_chunk(index)
        halves.append((exchange(passed, 0), held))

    row_weights, col_weights = pl.pallas_call(
        weight_kernel,
        out_shape=[
            jax.ShapeDtypeStruct((blocks, SUBW, NVIS), jnp.bfloat16),
            jax.ShapeDtypeStruct((blocks, SUBW, NVIS), jnp.float32),
        ],
        in_specs=[in_smem, in_vmem],
        out_specs=[in_vmem] * 2,
        compiler_params=params,
        cost_estimate=cost(5500000000),
        name="weights",
    )(block_kernel, vis_cells)

    for bit in range(1, bits):
        for index in range(CHUNKS):
            passed, held = halved(*halves[index], bit)
            halves[index] = (exchange(passed, bit), held)

    pieces = []
    for index in range(CHUNKS):
        first, second = halves[index]
        parts = {0: (first + second).astype(jnp.bfloat16)}
        for step in range(1, pairs):
            parts[step] = lax.ppermute(parts[0], "pair", [(p, p ^ step) for p in range(pairs)])
        pieces += [parts[step] for step in range(pairs)]

    return pl.pallas_call(
        functools.partial(degrid_kernel, pairs),
        out_shape=jax.ShapeDtypeStruct((blocks, 2, NVIS), jnp.float32),
        in_specs=[in_smem] * 2 + [in_vmem] * (3 + len(pieces)),
        out_specs=in_vmem,
        scratch_shapes=[pltpu.VMEM((SG_WIDE * SUBW, 2 * SUBW), jnp.bfloat16)],
        compiler_params=params,
        cost_estimate=cost(3300000000),
        name="degrid",
    )(place, block_subgrid, row_weights, col_weights, table_chunked(), *pieces)


def solution(mesh):
    placed = (
        P(("groups", "wide"), None, "pair", None),
        P("groups", None, None),
        P(("groups", "wide", "pair")),
        P(("groups", "wide", "pair"), None),
        P(("groups", "wide", "pair"), None, None),
    )
    return jax.shard_map(
        on_device,
        mesh=mesh,
        in_specs=placed,
        out_specs=P(("groups", "wide", "pair"), None, None),
        check_vma=False,
    )
```

```python
import functools
import math

import jax
import jax.numpy as jnp
import ml_dtypes
import numpy as np
from jax import lax
from jax.experimental import pallas as pl
from jax.experimental.pallas import tpu as pltpu
from jax.sharding import PartitionSpec as P

L = 4096
SUBW = 256
NVIS = 2048
SUPPORT = 8
OVERSAMPLE = 16
SG_WIDE = 2
SHOWN = 2 * SG_WIDE
CHUNKS = 2
CW = SUBW // CHUNKS
LANES = 2 * CW
FINE = 16
WIDTH = 256
PARTS = 2
PART = LANES // PARTS
VMEM_LIMIT = 20 << 20

TURN = float(np.float32(2.0 * math.pi / L))
TURN_HIGH = float(np.float32(np.round(2.0 * math.pi / L * 2**20) / 2**20))
TURN_LOW = 2.0 * math.pi / L - TURN_HIGH


def tap_shape(fraction):
    centre = (SUPPORT - 1) / 2.0 + (fraction.astype(jnp.float32) + 0.5) / OVERSAMPLE - 0.5
    point = lax.broadcasted_iota(jnp.int32, (SUPPORT, 128), 0).astype(jnp.float32)
    distance = point - centre
    total = jnp.sum(jnp.exp(-distance * distance / 2.88), axis=0, keepdims=True)
    return centre, -jnp.log2(total)[:, 0:1]


def table_chunked():
    grid_ids = np.arange(SUBW)
    phase = 2.0 * math.pi / SUBW * (grid_ids[:, None] * grid_ids[None, :] % SUBW)
    cosine = np.cos(phase) / math.sqrt(SUBW)
    sine = np.sin(phase) / math.sqrt(SUBW)
    upper = np.concatenate([cosine, -sine], axis=1).reshape(CHUNKS, 1, CW, 2 * SUBW)
    lower = np.concatenate([sine, cosine], axis=1).reshape(CHUNKS, 1, CW, 2 * SUBW)
    both = np.concatenate([upper, lower], axis=1).reshape(2 * SUBW, 2 * SUBW)
    return jnp.asarray(both.T.astype(np.float32).astype(ml_dtypes.bfloat16))


def cos_sin(number):
    quarter = lax.shift_right_logical(number + L // 8, int(math.log2(L // 4)))
    angle = (number - quarter * (L // 4)).astype(jnp.float32) * TURN
    square = angle * angle
    sine = 1.0 / 362880
    for term in (-1.0 / 5040, 1.0 / 120, -1.0 / 6, 1.0):
        sine = sine * square + term
    sine = sine * angle
    cosine = -1.0 / 3628800
    for term in (1.0 / 40320, -1.0 / 720, 1.0 / 24, -0.5, 1.0):
        cosine = cosine * square + term
    odd = (quarter & 1) == 1
    first = jnp.where(odd, sine, cosine)
    second = jnp.where(odd, cosine, sine)
    first = jnp.where(((quarter + 1) & 2) == 2, -first, first)
    second = jnp.where((quarter & 2) == 2, -second, second)
    return first, second


def ramp_of(shift):
    lane = lax.broadcasted_iota(jnp.int32, (1, 2 * SUBW), 1)
    column = lane // LANES * CW + lane % CW
    cosine, sine = cos_sin((shift * column) % SUBW * (L // SUBW))
    return cosine, jnp.where(lane % LANES < CW, sine, -sine)


def cost(flops):
    return pl.CostEstimate(flops=flops, bytes_accessed=1 << 20, transcendentals=0)


def swap_halves(value):
    return jnp.concatenate([value[:, CW:], value[:, :CW]], axis=1)


def ramped(direct, crossed, cosine, sine):
    part = direct + jnp.concatenate([crossed[:, CW:], -crossed[:, :CW]], axis=1)
    return part * cosine + swap_halves(part) * sine


def shift_of(offset_ref, place_ref, wides, hop, shown, part):
    wide_id = place_ref[1]
    owner = wide_id ^ (shown // SG_WIDE)
    facet = lax.rem(wide_id - 2 * hop + wides, wides)
    return offset_ref[SG_WIDE * owner + shown % SG_WIDE, facet, part]


def prep_kernel(wides, offset_ref, place_ref, strips_hbm, rest_ref, *refs):
    own_refs = refs[:CHUNKS]
    fine, fine_at, base, base_at, held, strips_ref, arrival = refs[CHUNKS:]
    chips = wides // 2
    shift_at = functools.partial(shift_of, offset_ref, place_ref, wides)
    length = strips_ref.shape[1]
    copy = pltpu.make_async_copy(strips_hbm, strips_ref, arrival)
    copy.start()
    row_ids = place_ref[0] + lax.broadcasted_iota(jnp.int32, (FINE, length), 1)
    group = lax.broadcasted_iota(jnp.int32, (FINE, length), 0)
    centred = (2 * row_ids + 1).astype(jnp.float32) / L - 1.0
    taper = (1.0 - 0.5 * centred * centred) / math.sqrt(L)
    number = (group * row_ids) & (L - 1)
    fine_at[...] = number
    cosine, sine = cos_sin(number)
    fine[0] = cosine
    fine[1] = sine

    def make_factor(facet, shown, store):
        shift = shift_at(facet, shown, 0) + (L - SUBW // 2)
        number = ((shift + FINE * group) * row_ids) & (L - 1)
        base_at[...] = number
        cosine, sine = cos_sin(number)
        base[0] = cosine * taper
        base[1] = sine * taper

        def one_strip(step, carry):
            lanes = pl.ds(pl.multiple_of(step * WIDTH, WIDTH), WIDTH)
            fine_n = fine_at[:, lanes]
            fine_c = fine[0, :, lanes]
            fine_s = fine[1, :, lanes]
            for high in range(SUBW // FINE):
                at = (base_at[high : high + 1, lanes] + fine_n) & (L - 1)
                count = at.astype(jnp.float32)
                turned = count * TURN
                slip = (turned - count * TURN_HIGH) - count * TURN_LOW
                base_c = base[0, high : high + 1, lanes]
                base_s = base[1, high : high + 1, lanes]
                cosine = base_c * fine_c - base_s * fine_s
                sine = base_s * fine_c + base_c * fine_s
                store(
                    slice(high * FINE, (high + 1) * FINE),
                    step * WIDTH,
                    (cosine - slip * sine).astype(jnp.bfloat16),
                    (sine + slip * cosine).astype(jnp.bfloat16),
                )
            return carry

        lax.fori_loop(0, length // WIDTH, one_strip, 0)

    def rest_step(step, carry):
        facet = step // SHOWN
        shown = step % SHOWN

        def store(rows, start, cosine, sine):
            rest_ref[facet, shown, rows, pl.ds(pl.multiple_of(start, WIDTH), WIDTH)] = cosine
            rest_ref[facet, shown, rows, pl.ds(pl.multiple_of(start + length, WIDTH), WIDTH)] = sine

        make_factor(facet + 1, shown, store)
        return carry

    lax.fori_loop(0, (chips - 1) * SHOWN, rest_step, 0)
    copy.wait()

    def own_step(shown, carry):
        def store(rows, start, cosine, sine):
            held[rows, pl.ds(pl.multiple_of(start, WIDTH), WIDTH)] = cosine
            held[rows, pl.ds(pl.multiple_of(start + length, WIDTH), WIDTH)] = sine

        make_factor(0, shown, store)
        ramp_c, ramp_s = ramp_of(shift_at(0, shown, 1))
        for chunk in range(CHUNKS):
            columns = slice(chunk * CW, (chunk + 1) * CW)
            lanes = slice(chunk * LANES, (chunk + 1) * LANES)
            data = jnp.concatenate([strips_ref[0, :, columns], strips_ref[1, :, columns]], axis=1)
            direct = jnp.dot(held[:, :length], data, preferred_element_type=jnp.float32)
            crossed = jnp.dot(held[:, length:], data, preferred_element_type=jnp.float32)
            own_refs[chunk][shown] = ramped(direct, crossed, ramp_c[:, lanes], ramp_s[:, lanes])
        return carry

    lax.fori_loop(0, SHOWN, own_step, 0)


def chunk_kernel(chunk, wides, offset_ref, place_ref, rest_ref, own_ref, *refs):
    hops = wides // 2 - 1
    targets, whole = refs[-5:-1], refs[-1]
    rows_dev = targets[0].shape[-2]
    groups = SUBW // (2 * rows_dev)
    mine = place_ref[2] & 1
    lanes = slice(chunk * LANES, (chunk + 1) * LANES)
    length = refs[0].shape[1]
    for shown in range(SHOWN):
        total = own_ref[shown]
        for hop in range(hops):
            data = jnp.concatenate([refs[hop][0], refs[hop][1]], axis=1)
            ramp_c, ramp_s = ramp_of(shift_of(offset_ref, place_ref, wides, hop + 1, shown, 1))
            direct = jnp.dot(
                rest_ref[hop, shown, :, :length], data, preferred_element_type=jnp.float32
            )
            crossed = jnp.dot(
                rest_ref[hop, shown, :, length:], data, preferred_element_type=jnp.float32
            )
            total = total + ramped(direct, crossed, ramp_c[:, lanes], ramp_s[:, lanes])
        whole[...] = total
        for group in range(groups):
            index = shown % SG_WIDE * groups + group
            for half in range(2):
                side = mine ^ (1 - half)
                at = pl.multiple_of((2 * group + side) * rows_dev, rows_dev)
                for part in range(PARTS):
                    targets[shown // SG_WIDE * 2 + half][part, index] = whole[
                        pl.ds(at, rows_dev), part * PART : (part + 1) * PART
                    ]


def weight_kernel(fraction_ref, cells_ref, row_ref, col_ref):
    width = 512
    scale = -1.0 / (2.88 * math.log(2.0))
    ids = lax.broadcasted_iota(jnp.int32, (SUBW, width), 0).astype(jnp.float32)
    for block in range(cells_ref.shape[0]):
        for part, target in ((0, row_ref), (1, col_ref)):
            centre, norm = tap_shape(fraction_ref[block, part])

            def one_part(step, carry):
                lanes = pl.ds(pl.multiple_of(step * width, width), width)
                distance = ids - cells_ref[block, part : part + 1, lanes].astype(jnp.float32)
                offset = distance - centre
                values = jnp.exp2(offset * offset * scale + norm)
                inside = jnp.abs(distance - (SUPPORT - 1) / 2.0) < SUPPORT / 2.0
                target[block, :, lanes] = jnp.where(inside, values, 0.0).astype(target.dtype)
                return carry

            lax.fori_loop(0, NVIS // width, one_part, 0)


def degrid_kernel(pairs, place_ref, pick_ref, row_ref, col_ref, table_ref, *refs):
    count = CHUNKS * pairs
    pieces = refs[:count]
    out_ref, held = refs[count:]
    rows_dev = pieces[0].shape[1]
    place = place_ref[2]
    for chunk in range(CHUNKS):
        for step in range(pairs):
            at = pl.multiple_of((place ^ step) * rows_dev, rows_dev)
            for part in range(PARTS):
                lane = chunk * LANES + part * PART
                held[pl.ds(at, rows_dev), lane : lane + PART] = pieces[chunk * pairs + step][part]
    width = 512
    for block in range(row_ref.shape[0]):
        first = pl.multiple_of(pick_ref[block] * SUBW, SUBW)
        spectrum = lax.dot_general(
            table_ref[...],
            held[pl.ds(first, SUBW), :],
            (((1,), (1,)), ((), ())),
            preferred_element_type=jnp.float32,
        ).astype(jnp.bfloat16)
        for start in range(0, NVIS, width):
            lanes = slice(start, start + width)
            spread = jnp.dot(
                spectrum, row_ref[block, :, lanes], preferred_element_type=jnp.float32
            )
            weights = col_ref[block, :, lanes]
            out_ref[block, 0:1, lanes] = jnp.sum(weights * spread[:SUBW], axis=0, keepdims=True)
            out_ref[block, 1:2, lanes] = jnp.sum(weights * spread[SUBW:], axis=0, keepdims=True)


def on_device(strips, offsets, block_subgrid, block_kernel, vis_cells):
    pairs = lax.axis_size("pair")
    wides = lax.axis_size("wide")
    chips = wides // 2
    wide_id = lax.axis_index("wide")
    pair_id = lax.axis_index("pair")
    length = strips.shape[2]
    rows_dev = SG_WIDE * SUBW // pairs
    in_smem = pl.BlockSpec(memory_space=pltpu.SMEM)
    in_vmem = pl.BlockSpec(memory_space=pltpu.VMEM)
    anywhere = pl.BlockSpec(memory_space=pl.ANY)
    params = pltpu.CompilerParams(vmem_limit_bytes=VMEM_LIMIT)

    strips = strips[0]
    arrived = []
    for index in range(CHUNKS):
        part = strips[:, :, index * CW : (index + 1) * CW]
        arrived.append(
            [
                lax.ppermute(part, "wide", [(w, (w + 2 * hop) % wides) for w in range(wides)])
                for hop in range(1, chips)
            ]
        )

    place = jnp.stack([pair_id * length, wide_id, pair_id])

    rest, *own = pl.pallas_call(
        functools.partial(prep_kernel, wides),
        out_shape=[
            jax.ShapeDtypeStruct((chips - 1, SHOWN, SUBW, 2 * length), jnp.bfloat16),
        ]
        + [jax.ShapeDtypeStruct((SHOWN, SUBW, LANES), jnp.float32)] * CHUNKS,
        in_specs=[in_smem, in_smem, anywhere],
        out_specs=[in_vmem] * (1 + CHUNKS),
        scratch_shapes=[
            pltpu.VMEM((2, FINE, length), jnp.float32),
            pltpu.VMEM((FINE, length), jnp.int32),
            pltpu.VMEM((2, FINE, length), jnp.float32),
            pltpu.VMEM((FINE, length), jnp.int32),
            pltpu.VMEM((SUBW, 2 * length), jnp.bfloat16),
            pltpu.VMEM((2, length, SUBW), jnp.bfloat16),
            pltpu.SemaphoreType.DMA,
        ],
        compiler_params=params,
        cost_estimate=cost(12100000000),
        name="prepare",
    )(offsets, place, strips)

    bits = pairs.bit_length() - 1

    def start_chunk(index):
        sums = pl.pallas_call(
            functools.partial(chunk_kernel, index, wides),
            out_shape=[jax.ShapeDtypeStruct((PARTS, pairs // 2, rows_dev, PART), jnp.float32)] * 4,
            in_specs=[in_smem, in_smem] + [in_vmem] * (chips + 1),
            out_specs=[in_vmem] * 4,
            scratch_shapes=[pltpu.VMEM((SUBW, LANES), jnp.float32)],
            compiler_params=params,
            cost_estimate=cost(2420000000),
            name="chunk_sums",
        )(offsets, place, rest, own[index], *arrived[index])
        shape = (2,) * (bits - 1) + (rows_dev, PART)
        cores = [(w, w ^ 1) for w in range(wides)]
        keep_pass, keep_hold, send_pass, send_hold = sums
        other_pass = lax.ppermute(send_pass, "wide", cores)
        other_hold = lax.ppermute(send_hold, "wide", cores)
        return [
            (
                (keep_pass[part] + other_pass[part]).reshape(shape),
                (keep_hold[part] + other_hold[part]).reshape(shape),
            )
            for part in range(PARTS)
        ]

    def halved(first, second, bit):
        axis = first.ndim - 3
        mine = (pair_id >> bit) & 1
        passed, held = [
            lax.dynamic_index_in_dim(first, side, axis, keepdims=False)
            + lax.dynamic_index_in_dim(second, side, axis, keepdims=False)
            for side in (1 - mine, mine)
        ]
        return passed, held

    def exchange(passed, bit):
        return lax.ppermute(passed, "pair", [(p, p ^ (1 << bit)) for p in range(pairs)])

    blocks = vis_cells.shape[0]
    halves = []
    for index in range(CHUNKS):
        for passed, held in start_chunk(index):
            halves.append((exchange(passed, 0), held))

    row_weights, col_weights = pl.pallas_call(
        weight_kernel,
        out_shape=[
            jax.ShapeDtypeStruct((blocks, SUBW, NVIS), jnp.bfloat16),
            jax.ShapeDtypeStruct((blocks, SUBW, NVIS), jnp.float32),
        ],
        in_specs=[in_smem, in_vmem],
        out_specs=[in_vmem] * 2,
        compiler_params=params,
        cost_estimate=cost(5500000000),
        name="weights",
    )(block_kernel, vis_cells)

    for bit in range(1, bits):
        for index in range(CHUNKS * PARTS):
            passed, held = halved(*halves[index], bit)
            halves[index] = (exchange(passed, bit), held)

    pieces = []
    for index in range(CHUNKS):
        both = halves[index * PARTS : (index + 1) * PARTS]
        parts = {0: jnp.stack([first + second for first, second in both]).astype(jnp.bfloat16)}
        for step in range(1, pairs):
            parts[step] = lax.ppermute(parts[0], "pair", [(p, p ^ step) for p in range(pairs)])
        pieces += [parts[step] for step in range(pairs)]

    return pl.pallas_call(
        functools.partial(degrid_kernel, pairs),
        out_shape=jax.ShapeDtypeStruct((blocks, 2, NVIS), jnp.float32),
        in_specs=[in_smem] * 2 + [in_vmem] * (3 + len(pieces)),
        out_specs=in_vmem,
        scratch_shapes=[pltpu.VMEM((SG_WIDE * SUBW, 2 * SUBW), jnp.bfloat16)],
        compiler_params=params,
        cost_estimate=cost(3300000000),
        name="degrid",
    )(place, block_subgrid, row_weights, col_weights, table_chunked(), *pieces)


def solution(mesh):
    placed = (
        P(("groups", "wide"), None, "pair", None),
        P("groups", None, None),
        P(("groups", "wide", "pair")),
        P(("groups", "wide", "pair"), None),
        P(("groups", "wide", "pair"), None, None),
    )
    return jax.shard_map(
        on_device,
        mesh=mesh,
        in_specs=placed,
        out_specs=P(("groups", "wide", "pair"), None, None),
        check_vma=False,
    )
```

```python
import functools
import math

import jax
import jax.numpy as jnp
import ml_dtypes
import numpy as np
from jax import lax
from jax.experimental import pallas as pl
from jax.experimental.pallas import tpu as pltpu
from jax.sharding import PartitionSpec as P

L = 4096
SUBW = 256
NVIS = 2048
SUPPORT = 8
OVERSAMPLE = 16
SG_WIDE = 2
SHOWN = 2 * SG_WIDE
CHUNKS = 2
CW = SUBW // CHUNKS
LANES = 2 * CW
FINE = 16
WIDTH = 256
PARTS = 2
PART = LANES // PARTS
VMEM_LIMIT = 20 << 20

TURN = float(np.float32(2.0 * math.pi / L))
TURN_HIGH = float(np.float32(np.round(2.0 * math.pi / L * 2**20) / 2**20))
TURN_LOW = 2.0 * math.pi / L - TURN_HIGH


def tap_shape(fraction):
    centre = (SUPPORT - 1) / 2.0 + (fraction.astype(jnp.float32) + 0.5) / OVERSAMPLE - 0.5
    point = lax.broadcasted_iota(jnp.int32, (SUPPORT, 128), 0).astype(jnp.float32)
    distance = point - centre
    total = jnp.sum(jnp.exp(-distance * distance / 2.88), axis=0, keepdims=True)
    return centre, -jnp.log2(total)[:, 0:1]


def table_chunked():
    grid_ids = np.arange(SUBW)
    phase = 2.0 * math.pi / SUBW * (grid_ids[:, None] * grid_ids[None, :] % SUBW)
    cosine = np.cos(phase) / math.sqrt(SUBW)
    sine = np.sin(phase) / math.sqrt(SUBW)
    upper = np.concatenate([cosine, -sine], axis=1).reshape(CHUNKS, 1, CW, 2 * SUBW)
    lower = np.concatenate([sine, cosine], axis=1).reshape(CHUNKS, 1, CW, 2 * SUBW)
    both = np.concatenate([upper, lower], axis=1).reshape(2 * SUBW, 2 * SUBW)
    return jnp.asarray(both.T.astype(np.float32).astype(ml_dtypes.bfloat16))


def cos_sin(number):
    quarter = lax.shift_right_logical(number + L // 8, int(math.log2(L // 4)))
    angle = (number - quarter * (L // 4)).astype(jnp.float32) * TURN
    square = angle * angle
    sine = 1.0 / 362880
    for term in (-1.0 / 5040, 1.0 / 120, -1.0 / 6, 1.0):
        sine = sine * square + term
    sine = sine * angle
    cosine = -1.0 / 3628800
    for term in (1.0 / 40320, -1.0 / 720, 1.0 / 24, -0.5, 1.0):
        cosine = cosine * square + term
    odd = (quarter & 1) == 1
    first = jnp.where(odd, sine, cosine)
    second = jnp.where(odd, cosine, sine)
    first = jnp.where(((quarter + 1) & 2) == 2, -first, first)
    second = jnp.where((quarter & 2) == 2, -second, second)
    return first, second


def ramp_of(shift):
    lane = lax.broadcasted_iota(jnp.int32, (1, 2 * SUBW), 1)
    column = lane // LANES * CW + lane % CW
    cosine, sine = cos_sin((shift * column) % SUBW * (L // SUBW))
    return cosine, jnp.where(lane % LANES < CW, sine, -sine)


def cost(flops):
    return pl.CostEstimate(flops=flops, bytes_accessed=1 << 20, transcendentals=0)


def swap_halves(value):
    return jnp.concatenate([value[:, CW:], value[:, :CW]], axis=1)


def ramped(direct, crossed, cosine, sine):
    part = direct + jnp.concatenate([crossed[:, CW:], -crossed[:, :CW]], axis=1)
    return part * cosine + swap_halves(part) * sine


def shift_of(offset_ref, place_ref, wides, hop, shown, part):
    wide_id = place_ref[1]
    owner = wide_id ^ (shown // SG_WIDE)
    facet = lax.rem(wide_id - 2 * hop + wides, wides)
    return offset_ref[SG_WIDE * owner + shown % SG_WIDE, facet, part]


def prep_kernel(wides, offset_ref, place_ref, strips_hbm, rest_ref, *refs):
    own_refs, ramp_ref = refs[:CHUNKS], refs[CHUNKS]
    fine, fine_at, base, base_at, held, strips_ref, arrival = refs[CHUNKS + 1 :]
    chips = wides // 2
    shift_at = functools.partial(shift_of, offset_ref, place_ref, wides)
    length = strips_ref.shape[1]
    copy = pltpu.make_async_copy(strips_hbm, strips_ref, arrival)
    copy.start()
    row_ids = place_ref[0] + lax.broadcasted_iota(jnp.int32, (FINE, length), 1)
    group = lax.broadcasted_iota(jnp.int32, (FINE, length), 0)
    centred = (2 * row_ids + 1).astype(jnp.float32) / L - 1.0
    taper = (1.0 - 0.5 * centred * centred) / math.sqrt(L)
    number = (group * row_ids) & (L - 1)
    fine_at[...] = number
    cosine, sine = cos_sin(number)
    fine[0] = cosine
    fine[1] = sine

    def make_factor(facet, shown, store):
        shift = shift_at(facet, shown, 0) + (L - SUBW // 2)
        number = ((shift + FINE * group) * row_ids) & (L - 1)
        base_at[...] = number
        cosine, sine = cos_sin(number)
        base[0] = cosine * taper
        base[1] = sine * taper

        def one_strip(step, carry):
            lanes = pl.ds(pl.multiple_of(step * WIDTH, WIDTH), WIDTH)
            fine_n = fine_at[:, lanes]
            fine_c = fine[0, :, lanes]
            fine_s = fine[1, :, lanes]
            for high in range(SUBW // FINE):
                at = (base_at[high : high + 1, lanes] + fine_n) & (L - 1)
                count = at.astype(jnp.float32)
                turned = count * TURN
                slip = (turned - count * TURN_HIGH) - count * TURN_LOW
                base_c = base[0, high : high + 1, lanes]
                base_s = base[1, high : high + 1, lanes]
                cosine = base_c * fine_c - base_s * fine_s
                sine = base_s * fine_c + base_c * fine_s
                store(
                    slice(high * FINE, (high + 1) * FINE),
                    step * WIDTH,
                    (cosine - slip * sine).astype(jnp.bfloat16),
                    (sine + slip * cosine).astype(jnp.bfloat16),
                )
            return carry

        lax.fori_loop(0, length // WIDTH, one_strip, 0)

    def rest_step(step, carry):
        facet = step // SHOWN
        shown = step % SHOWN

        def store(rows, start, cosine, sine):
            rest_ref[facet, shown, rows, pl.ds(pl.multiple_of(start, WIDTH), WIDTH)] = cosine
            rest_ref[facet, shown, rows, pl.ds(pl.multiple_of(start + length, WIDTH), WIDTH)] = sine

        ramp_c, ramp_s = ramp_of(shift_at(facet + 1, shown, 1))
        ramp_ref[facet, shown, 0:1] = ramp_c
        ramp_ref[facet, shown, 1:2] = ramp_s
        make_factor(facet + 1, shown, store)
        return carry

    lax.fori_loop(0, (chips - 1) * SHOWN, rest_step, 0)
    copy.wait()

    def own_step(shown, carry):
        def store(rows, start, cosine, sine):
            held[rows, pl.ds(pl.multiple_of(start, WIDTH), WIDTH)] = cosine
            held[rows, pl.ds(pl.multiple_of(start + length, WIDTH), WIDTH)] = sine

        make_factor(0, shown, store)
        ramp_c, ramp_s = ramp_of(shift_at(0, shown, 1))
        for chunk in range(CHUNKS):
            columns = slice(chunk * CW, (chunk + 1) * CW)
            lanes = slice(chunk * LANES, (chunk + 1) * LANES)
            data = jnp.concatenate([strips_ref[0, :, columns], strips_ref[1, :, columns]], axis=1)
            direct = jnp.dot(held[:, :length], data, preferred_element_type=jnp.float32)
            crossed = jnp.dot(held[:, length:], data, preferred_element_type=jnp.float32)
            own_refs[chunk][shown] = ramped(direct, crossed, ramp_c[:, lanes], ramp_s[:, lanes])
        return carry

    lax.fori_loop(0, SHOWN, own_step, 0)


def chunk_kernel(chunk, wides, place_ref, rest_ref, ramp_ref, own_ref, *refs):
    hops = wides // 2 - 1
    targets, whole = refs[-5:-1], refs[-1]
    rows_dev = targets[0].shape[-2]
    groups = SUBW // (2 * rows_dev)
    mine = place_ref[2] & 1
    lanes = slice(chunk * LANES, (chunk + 1) * LANES)
    stacked = [
        jnp.concatenate(
            [
                jnp.concatenate([refs[hop][0], refs[hop][1]], axis=1),
                jnp.concatenate([refs[hop][1], -refs[hop][0]], axis=1),
            ],
            axis=0,
        )
        for hop in range(hops)
    ]
    for shown in range(SHOWN):
        total = own_ref[shown]
        for hop in range(hops):
            ramp_c = ramp_ref[hop, shown, 0:1, lanes]
            ramp_s = ramp_ref[hop, shown, 1:2, lanes]
            part = jnp.dot(rest_ref[hop, shown], stacked[hop], preferred_element_type=jnp.float32)
            total = total + part * ramp_c + swap_halves(part) * ramp_s
        whole[...] = total
        for group in range(groups):
            index = shown % SG_WIDE * groups + group
            for half in range(2):
                side = mine ^ (1 - half)
                at = pl.multiple_of((2 * group + side) * rows_dev, rows_dev)
                for part in range(PARTS):
                    targets[shown // SG_WIDE * 2 + half][part, index] = whole[
                        pl.ds(at, rows_dev), part * PART : (part + 1) * PART
                    ]


def weight_kernel(fraction_ref, cells_ref, row_ref, col_ref):
    width = 512
    scale = -1.0 / (2.88 * math.log(2.0))
    ids = lax.broadcasted_iota(jnp.int32, (SUBW, width), 0).astype(jnp.float32)
    for block in range(cells_ref.shape[0]):
        for part, target in ((0, row_ref), (1, col_ref)):
            centre, norm = tap_shape(fraction_ref[block, part])

            def one_part(step, carry):
                lanes = pl.ds(pl.multiple_of(step * width, width), width)
                distance = ids - cells_ref[block, part : part + 1, lanes].astype(jnp.float32)
                offset = distance - centre
                values = jnp.exp2(offset * offset * scale + norm)
                inside = jnp.abs(distance - (SUPPORT - 1) / 2.0) < SUPPORT / 2.0
                target[block, :, lanes] = jnp.where(inside, values, 0.0).astype(target.dtype)
                return carry

            lax.fori_loop(0, NVIS // width, one_part, 0)


def degrid_kernel(pairs, place_ref, pick_ref, row_ref, col_ref, table_ref, *refs):
    count = CHUNKS * pairs
    pieces = refs[:count]
    out_ref, held = refs[count:]
    rows_dev = pieces[0].shape[1]
    place = place_ref[2]
    for chunk in range(CHUNKS):
        for step in range(pairs):
            at = pl.multiple_of((place ^ step) * rows_dev, rows_dev)
            for part in range(PARTS):
                lane = chunk * LANES + part * PART
                held[pl.ds(at, rows_dev), lane : lane + PART] = pieces[chunk * pairs + step][part]
    width = 512
    for block in range(row_ref.shape[0]):
        first = pl.multiple_of(pick_ref[block] * SUBW, SUBW)
        spectrum = lax.dot_general(
            table_ref[...],
            held[pl.ds(first, SUBW), :],
            (((1,), (1,)), ((), ())),
            preferred_element_type=jnp.float32,
        ).astype(jnp.bfloat16)
        for start in range(0, NVIS, width):
            lanes = slice(start, start + width)
            spread = jnp.dot(
                spectrum, row_ref[block, :, lanes], preferred_element_type=jnp.float32
            )
            weights = col_ref[block, :, lanes]
            out_ref[block, 0:1, lanes] = jnp.sum(weights * spread[:SUBW], axis=0, keepdims=True)
            out_ref[block, 1:2, lanes] = jnp.sum(weights * spread[SUBW:], axis=0, keepdims=True)


def on_device(strips, offsets, block_subgrid, block_kernel, vis_cells):
    pairs = lax.axis_size("pair")
    wides = lax.axis_size("wide")
    chips = wides // 2
    wide_id = lax.axis_index("wide")
    pair_id = lax.axis_index("pair")
    length = strips.shape[2]
    rows_dev = SG_WIDE * SUBW // pairs
    in_smem = pl.BlockSpec(memory_space=pltpu.SMEM)
    in_vmem = pl.BlockSpec(memory_space=pltpu.VMEM)
    anywhere = pl.BlockSpec(memory_space=pl.ANY)
    params = pltpu.CompilerParams(vmem_limit_bytes=VMEM_LIMIT)

    strips = strips[0]
    arrived = []
    for index in range(CHUNKS):
        part = strips[:, :, index * CW : (index + 1) * CW]
        arrived.append(
            [
                lax.ppermute(part, "wide", [(w, (w + 2 * hop) % wides) for w in range(wides)])
                for hop in range(1, chips)
            ]
        )

    place = jnp.stack([pair_id * length, wide_id, pair_id])

    rest, *own, ramps = pl.pallas_call(
        functools.partial(prep_kernel, wides),
        out_shape=[
            jax.ShapeDtypeStruct((chips - 1, SHOWN, SUBW, 2 * length), jnp.bfloat16),
        ]
        + [jax.ShapeDtypeStruct((SHOWN, SUBW, LANES), jnp.float32)] * CHUNKS
        + [jax.ShapeDtypeStruct((chips - 1, SHOWN, 2, 2 * SUBW), jnp.float32)],
        in_specs=[in_smem, in_smem, anywhere],
        out_specs=[in_vmem] * (2 + CHUNKS),
        scratch_shapes=[
            pltpu.VMEM((2, FINE, length), jnp.float32),
            pltpu.VMEM((FINE, length), jnp.int32),
            pltpu.VMEM((2, FINE, length), jnp.float32),
            pltpu.VMEM((FINE, length), jnp.int32),
            pltpu.VMEM((SUBW, 2 * length), jnp.bfloat16),
            pltpu.VMEM((2, length, SUBW), jnp.bfloat16),
            pltpu.SemaphoreType.DMA,
        ],
        compiler_params=params,
        cost_estimate=cost(12100000000),
        name="prepare",
    )(offsets, place, strips)

    bits = pairs.bit_length() - 1

    def start_chunk(index):
        sums = pl.pallas_call(
            functools.partial(chunk_kernel, index, wides),
            out_shape=[jax.ShapeDtypeStruct((PARTS, pairs // 2, rows_dev, PART), jnp.float32)] * 4,
            in_specs=[in_smem] + [in_vmem] * (chips + 2),
            out_specs=[in_vmem] * 4,
            scratch_shapes=[pltpu.VMEM((SUBW, LANES), jnp.float32)],
            compiler_params=params,
            cost_estimate=cost(2420000000),
            name="chunk_sums",
        )(place, rest, ramps, own[index], *arrived[index])
        shape = (2,) * (bits - 1) + (rows_dev, PART)
        cores = [(w, w ^ 1) for w in range(wides)]
        keep_pass, keep_hold, send_pass, send_hold = sums
        other_pass = lax.ppermute(send_pass, "wide", cores)
        other_hold = lax.ppermute(send_hold, "wide", cores)
        return [
            (
                (keep_pass[part] + other_pass[part]).reshape(shape),
                (keep_hold[part] + other_hold[part]).reshape(shape),
            )
            for part in range(PARTS)
        ]

    def halved(first, second, bit):
        axis = first.ndim - 3
        mine = (pair_id >> bit) & 1
        passed, held = [
            lax.dynamic_index_in_dim(first, side, axis, keepdims=False)
            + lax.dynamic_index_in_dim(second, side, axis, keepdims=False)
            for side in (1 - mine, mine)
        ]
        return passed, held

    def exchange(passed, bit):
        return lax.ppermute(passed, "pair", [(p, p ^ (1 << bit)) for p in range(pairs)])

    blocks = vis_cells.shape[0]
    halves = []
    for index in range(CHUNKS):
        for passed, held in start_chunk(index):
            halves.append((exchange(passed, 0), held))

    row_weights, col_weights = pl.pallas_call(
        weight_kernel,
        out_shape=[
            jax.ShapeDtypeStruct((blocks, SUBW, NVIS), jnp.bfloat16),
            jax.ShapeDtypeStruct((blocks, SUBW, NVIS), jnp.float32),
        ],
        in_specs=[in_smem, in_vmem],
        out_specs=[in_vmem] * 2,
        compiler_params=params,
        cost_estimate=cost(5500000000),
        name="weights",
    )(block_kernel, vis_cells)

    for bit in range(1, bits):
        for index in range(CHUNKS * PARTS):
            passed, held = halved(*halves[index], bit)
            halves[index] = (exchange(passed, bit), held)

    pieces = []
    for index in range(CHUNKS):
        both = halves[index * PARTS : (index + 1) * PARTS]
        parts = {0: jnp.stack([first + second for first, second in both]).astype(jnp.bfloat16)}
        for step in range(1, pairs):
            parts[step] = lax.ppermute(parts[0], "pair", [(p, p ^ step) for p in range(pairs)])
        pieces += [parts[step] for step in range(pairs)]

    return pl.pallas_call(
        functools.partial(degrid_kernel, pairs),
        out_shape=jax.ShapeDtypeStruct((blocks, 2, NVIS), jnp.float32),
        in_specs=[in_smem] * 2 + [in_vmem] * (3 + len(pieces)),
        out_specs=in_vmem,
        scratch_shapes=[pltpu.VMEM((SG_WIDE * SUBW, 2 * SUBW), jnp.bfloat16)],
        compiler_params=params,
        cost_estimate=cost(3300000000),
        name="degrid",
    )(place, block_subgrid, row_weights, col_weights, table_chunked(), *pieces)


def solution(mesh):
    placed = (
        P(("groups", "wide"), None, "pair", None),
        P("groups", None, None),
        P(("groups", "wide", "pair")),
        P(("groups", "wide", "pair"), None),
        P(("groups", "wide", "pair"), None, None),
    )
    return jax.shard_map(
        on_device,
        mesh=mesh,
        in_specs=placed,
        out_specs=P(("groups", "wide", "pair"), None, None),
        check_vma=False,
    )
```

```python
import functools
import math

import jax
import jax.numpy as jnp
import ml_dtypes
import numpy as np
from jax import lax
from jax.experimental import pallas as pl
from jax.experimental.pallas import tpu as pltpu
from jax.sharding import PartitionSpec as P

L = 4096
SUBW = 256
NVIS = 2048
SUPPORT = 8
OVERSAMPLE = 16
SG_WIDE = 2
SHOWN = 2 * SG_WIDE
CHUNKS = 2
CW = SUBW // CHUNKS
LANES = 2 * CW
FINE = 16
WIDTH = 256
PARTS = 2
PART = LANES // PARTS
VMEM_LIMIT = 20 << 20

TURN = float(np.float32(2.0 * math.pi / L))
TURN_HIGH = float(np.float32(np.round(2.0 * math.pi / L * 2**20) / 2**20))
TURN_LOW = 2.0 * math.pi / L - TURN_HIGH


def tap_shape(fraction):
    centre = (SUPPORT - 1) / 2.0 + (fraction.astype(jnp.float32) + 0.5) / OVERSAMPLE - 0.5
    point = lax.broadcasted_iota(jnp.int32, (SUPPORT, 128), 0).astype(jnp.float32)
    distance = point - centre
    total = jnp.sum(jnp.exp(-distance * distance / 2.88), axis=0, keepdims=True)
    return centre, -jnp.log2(total)[:, 0:1]


def table_chunked():
    grid_ids = np.arange(SUBW)
    phase = 2.0 * math.pi / SUBW * (grid_ids[:, None] * grid_ids[None, :] % SUBW)
    cosine = np.cos(phase) / math.sqrt(SUBW)
    sine = np.sin(phase) / math.sqrt(SUBW)
    upper = np.concatenate([cosine, -sine], axis=1).reshape(CHUNKS, 1, CW, 2 * SUBW)
    lower = np.concatenate([sine, cosine], axis=1).reshape(CHUNKS, 1, CW, 2 * SUBW)
    both = np.concatenate([upper, lower], axis=1).reshape(2 * SUBW, 2 * SUBW)
    return jnp.asarray(both.T.astype(np.float32).astype(ml_dtypes.bfloat16))


def cos_sin(number):
    quarter = lax.shift_right_logical(number + L // 8, int(math.log2(L // 4)))
    angle = (number - quarter * (L // 4)).astype(jnp.float32) * TURN
    square = angle * angle
    sine = 1.0 / 362880
    for term in (-1.0 / 5040, 1.0 / 120, -1.0 / 6, 1.0):
        sine = sine * square + term
    sine = sine * angle
    cosine = -1.0 / 3628800
    for term in (1.0 / 40320, -1.0 / 720, 1.0 / 24, -0.5, 1.0):
        cosine = cosine * square + term
    odd = (quarter & 1) == 1
    first = jnp.where(odd, sine, cosine)
    second = jnp.where(odd, cosine, sine)
    first = jnp.where(((quarter + 1) & 2) == 2, -first, first)
    second = jnp.where((quarter & 2) == 2, -second, second)
    return first, second


def ramp_of(shift):
    lane = lax.broadcasted_iota(jnp.int32, (1, 2 * SUBW), 1)
    column = lane // LANES * CW + lane % CW
    cosine, sine = cos_sin((shift * column) % SUBW * (L // SUBW))
    return cosine, jnp.where(lane % LANES < CW, sine, -sine)


def cost(flops):
    return pl.CostEstimate(flops=flops, bytes_accessed=1 << 20, transcendentals=0)


def swap_halves(value):
    return jnp.concatenate([value[:, CW:], value[:, :CW]], axis=1)


def ramped(direct, crossed, cosine, sine):
    part = direct + jnp.concatenate([crossed[:, CW:], -crossed[:, :CW]], axis=1)
    return part * cosine + swap_halves(part) * sine


def shift_of(offset_ref, place_ref, wides, hop, shown, part):
    wide_id = place_ref[1]
    owner = wide_id ^ (shown // SG_WIDE)
    facet = lax.rem(wide_id - 2 * hop + wides, wides)
    return offset_ref[SG_WIDE * owner + shown % SG_WIDE, facet, part]


def prep_kernel(wides, offset_ref, place_ref, strips_hbm, rest_ref, *refs):
    own_refs, ramp_ref = refs[:CHUNKS], refs[CHUNKS]
    fine, fine_at, base, base_at, held, strips_ref, arrival = refs[CHUNKS + 1 :]
    chips = wides // 2
    shift_at = functools.partial(shift_of, offset_ref, place_ref, wides)
    length = strips_ref.shape[1]
    copy = pltpu.make_async_copy(strips_hbm, strips_ref, arrival)
    copy.start()
    row_ids = place_ref[0] + lax.broadcasted_iota(jnp.int32, (FINE, length), 1)
    group = lax.broadcasted_iota(jnp.int32, (FINE, length), 0)
    centred = (2 * row_ids + 1).astype(jnp.float32) / L - 1.0
    taper = (1.0 - 0.5 * centred * centred) / math.sqrt(L)
    number = (group * row_ids) & (L - 1)
    fine_at[...] = number
    cosine, sine = cos_sin(number)
    fine[0] = cosine
    fine[1] = sine

    def make_factor(facet, shown, store):
        shift = shift_at(facet, shown, 0) + (L - SUBW // 2)
        number = ((shift + FINE * group) * row_ids) & (L - 1)
        base_at[...] = number
        cosine, sine = cos_sin(number)
        base[0] = cosine * taper
        base[1] = sine * taper

        def one_strip(step, carry):
            lanes = pl.ds(pl.multiple_of(step * WIDTH, WIDTH), WIDTH)
            fine_n = fine_at[:, lanes]
            fine_c = fine[0, :, lanes]
            fine_s = fine[1, :, lanes]
            for high in range(SUBW // FINE):
                at = (base_at[high : high + 1, lanes] + fine_n) & (L - 1)
                count = at.astype(jnp.float32)
                turned = count * TURN
                slip = (turned - count * TURN_HIGH) - count * TURN_LOW
                base_c = base[0, high : high + 1, lanes]
                base_s = base[1, high : high + 1, lanes]
                cosine = base_c * fine_c - base_s * fine_s
                sine = base_s * fine_c + base_c * fine_s
                store(
                    slice(high * FINE, (high + 1) * FINE),
                    step * WIDTH,
                    (cosine - slip * sine).astype(jnp.bfloat16),
                    (sine + slip * cosine).astype(jnp.bfloat16),
                )
            return carry

        lax.fori_loop(0, length // WIDTH, one_strip, 0)

    def rest_step(step, carry):
        facet = step // SHOWN
        shown = step % SHOWN

        def store(rows, start, cosine, sine):
            rest_ref[facet, shown, rows, pl.ds(pl.multiple_of(start, WIDTH), WIDTH)] = cosine
            rest_ref[facet, shown, rows, pl.ds(pl.multiple_of(start + length, WIDTH), WIDTH)] = sine

        ramp_c, ramp_s = ramp_of(shift_at(facet + 1, shown, 1))
        ramp_ref[facet, shown, 0:1] = ramp_c
        ramp_ref[facet, shown, 1:2] = ramp_s
        make_factor(facet + 1, shown, store)
        return carry

    lax.fori_loop(0, (chips - 1) * SHOWN, rest_step, 0)
    copy.wait()

    def own_step(shown, carry):
        def store(rows, start, cosine, sine):
            held[rows, pl.ds(pl.multiple_of(start, WIDTH), WIDTH)] = cosine
            held[rows, pl.ds(pl.multiple_of(start + length, WIDTH), WIDTH)] = sine

        make_factor(0, shown, store)
        ramp_c, ramp_s = ramp_of(shift_at(0, shown, 1))
        for chunk in range(CHUNKS):
            columns = slice(chunk * CW, (chunk + 1) * CW)
            lanes = slice(chunk * LANES, (chunk + 1) * LANES)
            data = jnp.concatenate([strips_ref[0, :, columns], strips_ref[1, :, columns]], axis=1)
            direct = jnp.dot(held[:, :length], data, preferred_element_type=jnp.float32)
            crossed = jnp.dot(held[:, length:], data, preferred_element_type=jnp.float32)
            own_refs[chunk][shown] = ramped(direct, crossed, ramp_c[:, lanes], ramp_s[:, lanes])
        return carry

    lax.fori_loop(0, SHOWN, own_step, 0)


def chunk_kernel(chunk, wides, place_ref, rest_ref, ramp_ref, own_ref, *refs):
    hops = wides // 2 - 1
    targets = refs[-4:]
    rows_dev = targets[0].shape[-2]
    groups = SUBW // (2 * rows_dev)
    mine = place_ref[2] & 1
    lanes = slice(chunk * LANES, (chunk + 1) * LANES)
    stacked = [
        jnp.concatenate(
            [
                jnp.concatenate([refs[hop][0], refs[hop][1]], axis=1),
                jnp.concatenate([refs[hop][1], -refs[hop][0]], axis=1),
            ],
            axis=0,
        )
        for hop in range(hops)
    ]
    for shown in range(SHOWN):
        total = own_ref[shown]
        for hop in range(hops):
            ramp_c = ramp_ref[hop, shown, 0:1, lanes]
            ramp_s = ramp_ref[hop, shown, 1:2, lanes]
            part = jnp.dot(rest_ref[hop, shown], stacked[hop], preferred_element_type=jnp.float32)
            total = total + part * ramp_c + swap_halves(part) * ramp_s
        for group in range(groups):
            index = shown % SG_WIDE * groups + group
            low, high = [
                total[(2 * group + side) * rows_dev : (2 * group + side + 1) * rows_dev]
                for side in range(2)
            ]
            for half, value in enumerate((jnp.where(mine == 1, low, high), jnp.where(mine == 1, high, low))):
                for part in range(PARTS):
                    targets[shown // SG_WIDE * 2 + half][part, index] = value[
                        :, part * PART : (part + 1) * PART
                    ]


def weight_kernel(fraction_ref, cells_ref, row_ref, col_ref):
    width = 512
    scale = -1.0 / (2.88 * math.log(2.0))
    ids = lax.broadcasted_iota(jnp.int32, (SUBW, width), 0).astype(jnp.float32)
    for block in range(cells_ref.shape[0]):
        for part, target in ((0, row_ref), (1, col_ref)):
            centre, norm = tap_shape(fraction_ref[block, part])

            def one_part(step, carry):
                lanes = pl.ds(pl.multiple_of(step * width, width), width)
                distance = ids - cells_ref[block, part : part + 1, lanes].astype(jnp.float32)
                offset = distance - centre
                values = jnp.exp2(offset * offset * scale + norm)
                inside = jnp.abs(distance - (SUPPORT - 1) / 2.0) < SUPPORT / 2.0
                target[block, :, lanes] = jnp.where(inside, values, 0.0).astype(target.dtype)
                return carry

            lax.fori_loop(0, NVIS // width, one_part, 0)


def degrid_kernel(pairs, place_ref, pick_ref, row_ref, col_ref, table_ref, *refs):
    count = CHUNKS * pairs
    pieces = refs[:count]
    out_ref, held = refs[count:]
    rows_dev = pieces[0].shape[1]
    place = place_ref[2]
    for chunk in range(CHUNKS):
        for step in range(pairs):
            at = pl.multiple_of((place ^ step) * rows_dev, rows_dev)
            for part in range(PARTS):
                lane = chunk * LANES + part * PART
                held[pl.ds(at, rows_dev), lane : lane + PART] = pieces[chunk * pairs + step][part]
    width = 512
    for block in range(row_ref.shape[0]):
        first = pl.multiple_of(pick_ref[block] * SUBW, SUBW)
        spectrum = lax.dot_general(
            table_ref[...],
            held[pl.ds(first, SUBW), :],
            (((1,), (1,)), ((), ())),
            preferred_element_type=jnp.float32,
        ).astype(jnp.bfloat16)
        for start in range(0, NVIS, width):
            lanes = slice(start, start + width)
            spread = jnp.dot(
                spectrum, row_ref[block, :, lanes], preferred_element_type=jnp.float32
            )
            weights = col_ref[block, :, lanes]
            out_ref[block, 0:1, lanes] = jnp.sum(weights * spread[:SUBW], axis=0, keepdims=True)
            out_ref[block, 1:2, lanes] = jnp.sum(weights * spread[SUBW:], axis=0, keepdims=True)


def on_device(strips, offsets, block_subgrid, block_kernel, vis_cells):
    pairs = lax.axis_size("pair")
    wides = lax.axis_size("wide")
    chips = wides // 2
    wide_id = lax.axis_index("wide")
    pair_id = lax.axis_index("pair")
    length = strips.shape[2]
    rows_dev = SG_WIDE * SUBW // pairs
    in_smem = pl.BlockSpec(memory_space=pltpu.SMEM)
    in_vmem = pl.BlockSpec(memory_space=pltpu.VMEM)
    anywhere = pl.BlockSpec(memory_space=pl.ANY)
    params = pltpu.CompilerParams(vmem_limit_bytes=VMEM_LIMIT)

    strips = strips[0]
    arrived = []
    for index in range(CHUNKS):
        part = strips[:, :, index * CW : (index + 1) * CW]
        arrived.append(
            [
                lax.ppermute(part, "wide", [(w, (w + 2 * hop) % wides) for w in range(wides)])
                for hop in range(1, chips)
            ]
        )

    place = jnp.stack([pair_id * length, wide_id, pair_id])

    rest, *own, ramps = pl.pallas_call(
        functools.partial(prep_kernel, wides),
        out_shape=[
            jax.ShapeDtypeStruct((chips - 1, SHOWN, SUBW, 2 * length), jnp.bfloat16),
        ]
        + [jax.ShapeDtypeStruct((SHOWN, SUBW, LANES), jnp.float32)] * CHUNKS
        + [jax.ShapeDtypeStruct((chips - 1, SHOWN, 2, 2 * SUBW), jnp.float32)],
        in_specs=[in_smem, in_smem, anywhere],
        out_specs=[in_vmem] * (2 + CHUNKS),
        scratch_shapes=[
            pltpu.VMEM((2, FINE, length), jnp.float32),
            pltpu.VMEM((FINE, length), jnp.int32),
            pltpu.VMEM((2, FINE, length), jnp.float32),
            pltpu.VMEM((FINE, length), jnp.int32),
            pltpu.VMEM((SUBW, 2 * length), jnp.bfloat16),
            pltpu.VMEM((2, length, SUBW), jnp.bfloat16),
            pltpu.SemaphoreType.DMA,
        ],
        compiler_params=params,
        cost_estimate=cost(12100000000),
        name="prepare",
    )(offsets, place, strips)

    bits = pairs.bit_length() - 1

    def start_chunk(index):
        sums = pl.pallas_call(
            functools.partial(chunk_kernel, index, wides),
            out_shape=[jax.ShapeDtypeStruct((PARTS, pairs // 2, rows_dev, PART), jnp.float32)] * 4,
            in_specs=[in_smem] + [in_vmem] * (chips + 2),
            out_specs=[in_vmem] * 4,
            compiler_params=params,
            cost_estimate=cost(2420000000),
            name="chunk_sums",
        )(place, rest, ramps, own[index], *arrived[index])
        shape = (2,) * (bits - 1) + (rows_dev, PART)
        cores = [(w, w ^ 1) for w in range(wides)]
        keep_pass, keep_hold, send_pass, send_hold = sums
        other_pass = lax.ppermute(send_pass, "wide", cores)
        other_hold = lax.ppermute(send_hold, "wide", cores)
        return [
            (
                (keep_pass[part] + other_pass[part]).reshape(shape),
                (keep_hold[part] + other_hold[part]).reshape(shape),
            )
            for part in range(PARTS)
        ]

    def halved(first, second, bit):
        axis = first.ndim - 3
        mine = (pair_id >> bit) & 1
        passed, held = [
            lax.dynamic_index_in_dim(first, side, axis, keepdims=False)
            + lax.dynamic_index_in_dim(second, side, axis, keepdims=False)
            for side in (1 - mine, mine)
        ]
        return passed, held

    def exchange(passed, bit):
        return lax.ppermute(passed, "pair", [(p, p ^ (1 << bit)) for p in range(pairs)])

    blocks = vis_cells.shape[0]
    halves = []
    for index in range(CHUNKS):
        for passed, held in start_chunk(index):
            halves.append((exchange(passed, 0), held))

    row_weights, col_weights = pl.pallas_call(
        weight_kernel,
        out_shape=[
            jax.ShapeDtypeStruct((blocks, SUBW, NVIS), jnp.bfloat16),
            jax.ShapeDtypeStruct((blocks, SUBW, NVIS), jnp.float32),
        ],
        in_specs=[in_smem, in_vmem],
        out_specs=[in_vmem] * 2,
        compiler_params=params,
        cost_estimate=cost(5500000000),
        name="weights",
    )(block_kernel, vis_cells)

    for bit in range(1, bits):
        for index in range(CHUNKS * PARTS):
            passed, held = halved(*halves[index], bit)
            halves[index] = (exchange(passed, bit), held)

    pieces = []
    for index in range(CHUNKS):
        both = halves[index * PARTS : (index + 1) * PARTS]
        parts = {0: jnp.stack([first + second for first, second in both]).astype(jnp.bfloat16)}
        for step in range(1, pairs):
            parts[step] = lax.ppermute(parts[0], "pair", [(p, p ^ step) for p in range(pairs)])
        pieces += [parts[step] for step in range(pairs)]

    return pl.pallas_call(
        functools.partial(degrid_kernel, pairs),
        out_shape=jax.ShapeDtypeStruct((blocks, 2, NVIS), jnp.float32),
        in_specs=[in_smem] * 2 + [in_vmem] * (3 + len(pieces)),
        out_specs=in_vmem,
        scratch_shapes=[pltpu.VMEM((SG_WIDE * SUBW, 2 * SUBW), jnp.bfloat16)],
        compiler_params=params,
        cost_estimate=cost(3300000000),
        name="degrid",
    )(place, block_subgrid, row_weights, col_weights, table_chunked(), *pieces)


def solution(mesh):
    placed = (
        P(("groups", "wide"), None, "pair", None),
        P("groups", None, None),
        P(("groups", "wide", "pair")),
        P(("groups", "wide", "pair"), None),
        P(("groups", "wide", "pair"), None, None),
    )
    return jax.shard_map(
        on_device,
        mesh=mesh,
        in_specs=placed,
        out_specs=P(("groups", "wide", "pair"), None, None),
        check_vma=False,
    )
```

```python
import functools
import math

import jax
import jax.numpy as jnp
import ml_dtypes
import numpy as np
from jax import lax
from jax.experimental import pallas as pl
from jax.experimental.pallas import tpu as pltpu
from jax.sharding import PartitionSpec as P

L = 4096
SUBW = 256
NVIS = 2048
SUPPORT = 8
OVERSAMPLE = 16
SG_WIDE = 2
SHOWN = 2 * SG_WIDE
CHUNKS = 2
CW = SUBW // CHUNKS
LANES = 2 * CW
FINE = 16
WIDTH = 256
PARTS = 2
PART = LANES // PARTS
VMEM_LIMIT = 20 << 20

TURN = float(np.float32(2.0 * math.pi / L))
TURN_HIGH = float(np.float32(np.round(2.0 * math.pi / L * 2**20) / 2**20))
TURN_LOW = 2.0 * math.pi / L - TURN_HIGH


def tap_shape(fraction):
    centre = (SUPPORT - 1) / 2.0 + (fraction.astype(jnp.float32) + 0.5) / OVERSAMPLE - 0.5
    point = lax.broadcasted_iota(jnp.int32, (SUPPORT, 128), 0).astype(jnp.float32)
    distance = point - centre
    total = jnp.sum(jnp.exp(-distance * distance / 2.88), axis=0, keepdims=True)
    return centre, -jnp.log2(total)[:, 0:1]


def table_chunked():
    grid_ids = np.arange(SUBW)
    phase = 2.0 * math.pi / SUBW * (grid_ids[:, None] * grid_ids[None, :] % SUBW)
    cosine = np.cos(phase) / math.sqrt(SUBW)
    sine = np.sin(phase) / math.sqrt(SUBW)
    upper = np.concatenate([cosine, -sine], axis=1).reshape(CHUNKS, 1, CW, 2 * SUBW)
    lower = np.concatenate([sine, cosine], axis=1).reshape(CHUNKS, 1, CW, 2 * SUBW)
    both = np.concatenate([upper, lower], axis=1).reshape(2 * SUBW, 2 * SUBW)
    return jnp.asarray(both.T.astype(np.float32).astype(ml_dtypes.bfloat16))


def cos_sin(number):
    quarter = lax.shift_right_logical(number + L // 8, int(math.log2(L // 4)))
    angle = (number - quarter * (L // 4)).astype(jnp.float32) * TURN
    square = angle * angle
    sine = 1.0 / 362880
    for term in (-1.0 / 5040, 1.0 / 120, -1.0 / 6, 1.0):
        sine = sine * square + term
    sine = sine * angle
    cosine = -1.0 / 3628800
    for term in (1.0 / 40320, -1.0 / 720, 1.0 / 24, -0.5, 1.0):
        cosine = cosine * square + term
    odd = (quarter & 1) == 1
    first = jnp.where(odd, sine, cosine)
    second = jnp.where(odd, cosine, sine)
    first = jnp.where(((quarter + 1) & 2) == 2, -first, first)
    second = jnp.where((quarter & 2) == 2, -second, second)
    return first, second


def ramp_of(shift):
    lane = lax.broadcasted_iota(jnp.int32, (1, 2 * SUBW), 1)
    column = lane // LANES * CW + lane % CW
    cosine, sine = cos_sin((shift * column) % SUBW * (L // SUBW))
    return cosine, jnp.where(lane % LANES < CW, sine, -sine)


def cost(flops):
    return pl.CostEstimate(flops=flops, bytes_accessed=1 << 20, transcendentals=0)


def swap_halves(value):
    return jnp.concatenate([value[:, CW:], value[:, :CW]], axis=1)


def ramped(direct, crossed, cosine, sine):
    part = direct + jnp.concatenate([crossed[:, CW:], -crossed[:, :CW]], axis=1)
    return part * cosine + swap_halves(part) * sine


def shift_of(offset_ref, place_ref, wides, hop, shown, part):
    wide_id = place_ref[1]
    owner = wide_id ^ (shown // SG_WIDE)
    facet = lax.rem(wide_id - 2 * hop + wides, wides)
    return offset_ref[SG_WIDE * owner + shown % SG_WIDE, facet, part]


def prep_kernel(wides, offset_ref, place_ref, strips_hbm, rest_ref, *refs):
    own_refs, ramp_ref = refs[:CHUNKS], refs[CHUNKS]
    fine, fine_at, base, base_at, held, strips_ref, arrival = refs[CHUNKS + 1 :]
    chips = wides // 2
    shift_at = functools.partial(shift_of, offset_ref, place_ref, wides)
    length = strips_ref.shape[1]
    copy = pltpu.make_async_copy(strips_hbm, strips_ref, arrival)
    copy.start()
    row_ids = place_ref[0] + lax.broadcasted_iota(jnp.int32, (FINE, length), 1)
    group = lax.broadcasted_iota(jnp.int32, (FINE, length), 0)
    centred = (2 * row_ids + 1).astype(jnp.float32) / L - 1.0
    taper = (1.0 - 0.5 * centred * centred) / math.sqrt(L)
    number = (group * row_ids) & (L - 1)
    fine_at[...] = number
    cosine, sine = cos_sin(number)
    fine[0] = cosine
    fine[1] = sine

    def make_factor(facet, shown, store):
        shift = shift_at(facet, shown, 0) + (L - SUBW // 2)
        number = ((shift + FINE * group) * row_ids) & (L - 1)
        base_at[...] = number
        cosine, sine = cos_sin(number)
        base[0] = cosine * taper
        base[1] = sine * taper

        def one_strip(step, carry):
            lanes = pl.ds(pl.multiple_of(step * WIDTH, WIDTH), WIDTH)
            fine_n = fine_at[:, lanes]
            fine_c = fine[0, :, lanes]
            fine_s = fine[1, :, lanes]
            for high in range(SUBW // FINE):
                at = (base_at[high : high + 1, lanes] + fine_n) & (L - 1)
                count = at.astype(jnp.float32)
                turned = count * TURN
                slip = (turned - count * TURN_HIGH) - count * TURN_LOW
                base_c = base[0, high : high + 1, lanes]
                base_s = base[1, high : high + 1, lanes]
                cosine = base_c * fine_c - base_s * fine_s
                sine = base_s * fine_c + base_c * fine_s
                store(
                    slice(high * FINE, (high + 1) * FINE),
                    step * WIDTH,
                    (cosine - slip * sine).astype(jnp.bfloat16),
                    (sine + slip * cosine).astype(jnp.bfloat16),
                )
            return carry

        lax.fori_loop(0, length // WIDTH, one_strip, 0)

    def rest_step(step, carry):
        facet = step // SHOWN
        shown = step % SHOWN

        def store(rows, start, cosine, sine):
            rest_ref[facet, shown, rows, pl.ds(pl.multiple_of(start, WIDTH), WIDTH)] = cosine
            rest_ref[facet, shown, rows, pl.ds(pl.multiple_of(start + length, WIDTH), WIDTH)] = sine

        ramp_c, ramp_s = ramp_of(shift_at(facet + 1, shown, 1))
        ramp_ref[facet, shown, 0:1] = ramp_c
        ramp_ref[facet, shown, 1:2] = ramp_s
        make_factor(facet + 1, shown, store)
        return carry

    lax.fori_loop(0, (chips - 1) * SHOWN, rest_step, 0)
    copy.wait()

    def own_step(shown, carry):
        def store(rows, start, cosine, sine):
            held[rows, pl.ds(pl.multiple_of(start, WIDTH), WIDTH)] = cosine
            held[rows, pl.ds(pl.multiple_of(start + length, WIDTH), WIDTH)] = sine

        make_factor(0, shown, store)
        ramp_c, ramp_s = ramp_of(shift_at(0, shown, 1))
        for chunk in range(CHUNKS):
            columns = slice(chunk * CW, (chunk + 1) * CW)
            lanes = slice(chunk * LANES, (chunk + 1) * LANES)
            data = jnp.concatenate([strips_ref[0, :, columns], strips_ref[1, :, columns]], axis=1)
            direct = jnp.dot(held[:, :length], data, preferred_element_type=jnp.float32)
            crossed = jnp.dot(held[:, length:], data, preferred_element_type=jnp.float32)
            own_refs[chunk][shown] = ramped(direct, crossed, ramp_c[:, lanes], ramp_s[:, lanes])
        return carry

    lax.fori_loop(0, SHOWN, own_step, 0)


def chunk_kernel(chunk, wides, place_ref, rest_ref, ramp_ref, own_ref, *refs):
    hops = wides // 2 - 1
    targets = refs[-4:]
    rows_dev = targets[0].shape[-2]
    groups = SUBW // (2 * rows_dev)
    mine = place_ref[2] & 1
    lanes = slice(chunk * LANES, (chunk + 1) * LANES)
    stacked = [
        jnp.concatenate(
            [
                jnp.concatenate([refs[hop][0], refs[hop][1]], axis=1),
                jnp.concatenate([refs[hop][1], -refs[hop][0]], axis=1),
            ],
            axis=0,
        )
        for hop in range(hops)
    ]
    for shown in range(SHOWN):
        total = own_ref[shown]
        for hop in range(hops):
            ramp_c = ramp_ref[hop, shown, 0:1, lanes]
            ramp_s = ramp_ref[hop, shown, 1:2, lanes]
            part = jnp.dot(rest_ref[hop, shown], stacked[hop], preferred_element_type=jnp.float32)
            total = total + part * ramp_c + swap_halves(part) * ramp_s
        for group in range(groups):
            index = shown % SG_WIDE * groups + group
            low, high = [
                total[(2 * group + side) * rows_dev : (2 * group + side + 1) * rows_dev]
                for side in range(2)
            ]
            for half, value in enumerate((jnp.where(mine == 1, low, high), jnp.where(mine == 1, high, low))):
                for part in range(PARTS):
                    targets[shown // SG_WIDE * 2 + half][part, index] = value[
                        :, part * PART : (part + 1) * PART
                    ]


def weight_kernel(fraction_ref, cells_ref, row_ref, col_ref):
    width = 512
    scale = -1.0 / (2.88 * math.log(2.0))
    half = (SUPPORT - 1) / 2.0
    ids = lax.broadcasted_iota(jnp.int32, (SUBW, width), 0).astype(jnp.float32)
    for block in range(cells_ref.shape[0]):
        for part, target in ((0, row_ref), (1, col_ref)):
            centre, norm = tap_shape(fraction_ref[block, part])

            def one_part(step, carry):
                lanes = pl.ds(pl.multiple_of(step * width, width), width)
                middle = cells_ref[block, part : part + 1, lanes].astype(jnp.float32) + half
                distance = ids - middle
                offset = distance - (centre - half)
                values = jnp.exp2(offset * offset * scale + norm)
                inside = jnp.abs(distance) < SUPPORT / 2.0
                target[block, :, lanes] = jnp.where(inside, values, 0.0).astype(target.dtype)
                return carry

            lax.fori_loop(0, NVIS // width, one_part, 0)


def degrid_kernel(pairs, place_ref, pick_ref, row_ref, col_ref, table_ref, *refs):
    count = CHUNKS * pairs
    pieces = refs[:count]
    out_ref, held = refs[count:]
    rows_dev = pieces[0].shape[1]
    place = place_ref[2]
    for chunk in range(CHUNKS):
        for step in range(pairs):
            at = pl.multiple_of((place ^ step) * rows_dev, rows_dev)
            for part in range(PARTS):
                lane = chunk * LANES + part * PART
                held[pl.ds(at, rows_dev), lane : lane + PART] = pieces[chunk * pairs + step][part]
    width = 512
    for block in range(row_ref.shape[0]):
        first = pl.multiple_of(pick_ref[block] * SUBW, SUBW)
        spectrum = lax.dot_general(
            table_ref[...],
            held[pl.ds(first, SUBW), :],
            (((1,), (1,)), ((), ())),
            preferred_element_type=jnp.float32,
        ).astype(jnp.bfloat16)
        for start in range(0, NVIS, width):
            lanes = slice(start, start + width)
            spread = jnp.dot(
                spectrum, row_ref[block, :, lanes], preferred_element_type=jnp.float32
            )
            weights = col_ref[block, :, lanes]
            out_ref[block, 0:1, lanes] = jnp.sum(weights * spread[:SUBW], axis=0, keepdims=True)
            out_ref[block, 1:2, lanes] = jnp.sum(weights * spread[SUBW:], axis=0, keepdims=True)


def on_device(strips, offsets, block_subgrid, block_kernel, vis_cells):
    pairs = lax.axis_size("pair")
    wides = lax.axis_size("wide")
    chips = wides // 2
    wide_id = lax.axis_index("wide")
    pair_id = lax.axis_index("pair")
    length = strips.shape[2]
    rows_dev = SG_WIDE * SUBW // pairs
    in_smem = pl.BlockSpec(memory_space=pltpu.SMEM)
    in_vmem = pl.BlockSpec(memory_space=pltpu.VMEM)
    anywhere = pl.BlockSpec(memory_space=pl.ANY)
    params = pltpu.CompilerParams(vmem_limit_bytes=VMEM_LIMIT)

    strips = strips[0]
    arrived = []
    for index in range(CHUNKS):
        part = strips[:, :, index * CW : (index + 1) * CW]
        arrived.append(
            [
                lax.ppermute(part, "wide", [(w, (w + 2 * hop) % wides) for w in range(wides)])
                for hop in range(1, chips)
            ]
        )

    place = jnp.stack([pair_id * length, wide_id, pair_id])

    rest, *own, ramps = pl.pallas_call(
        functools.partial(prep_kernel, wides),
        out_shape=[
            jax.ShapeDtypeStruct((chips - 1, SHOWN, SUBW, 2 * length), jnp.bfloat16),
        ]
        + [jax.ShapeDtypeStruct((SHOWN, SUBW, LANES), jnp.float32)] * CHUNKS
        + [jax.ShapeDtypeStruct((chips - 1, SHOWN, 2, 2 * SUBW), jnp.float32)],
        in_specs=[in_smem, in_smem, anywhere],
        out_specs=[in_vmem] * (2 + CHUNKS),
        scratch_shapes=[
            pltpu.VMEM((2, FINE, length), jnp.float32),
            pltpu.VMEM((FINE, length), jnp.int32),
            pltpu.VMEM((2, FINE, length), jnp.float32),
            pltpu.VMEM((FINE, length), jnp.int32),
            pltpu.VMEM((SUBW, 2 * length), jnp.bfloat16),
            pltpu.VMEM((2, length, SUBW), jnp.bfloat16),
            pltpu.SemaphoreType.DMA,
        ],
        compiler_params=params,
        cost_estimate=cost(12100000000),
        name="prepare",
    )(offsets, place, strips)

    bits = pairs.bit_length() - 1

    def start_chunk(index):
        sums = pl.pallas_call(
            functools.partial(chunk_kernel, index, wides),
            out_shape=[jax.ShapeDtypeStruct((PARTS, pairs // 2, rows_dev, PART), jnp.float32)] * 4,
            in_specs=[in_smem] + [in_vmem] * (chips + 2),
            out_specs=[in_vmem] * 4,
            compiler_params=params,
            cost_estimate=cost(2420000000),
            name="chunk_sums",
        )(place, rest, ramps, own[index], *arrived[index])
        shape = (2,) * (bits - 1) + (rows_dev, PART)
        cores = [(w, w ^ 1) for w in range(wides)]
        keep_pass, keep_hold, send_pass, send_hold = sums
        other_pass = lax.ppermute(send_pass, "wide", cores)
        other_hold = lax.ppermute(send_hold, "wide", cores)
        return [
            (
                (keep_pass[part] + other_pass[part]).reshape(shape),
                (keep_hold[part] + other_hold[part]).reshape(shape),
            )
            for part in range(PARTS)
        ]

    def halved(first, second, bit):
        axis = first.ndim - 3
        mine = (pair_id >> bit) & 1
        passed, held = [
            lax.dynamic_index_in_dim(first, side, axis, keepdims=False)
            + lax.dynamic_index_in_dim(second, side, axis, keepdims=False)
            for side in (1 - mine, mine)
        ]
        return passed, held

    def exchange(passed, bit):
        return lax.ppermute(passed, "pair", [(p, p ^ (1 << bit)) for p in range(pairs)])

    blocks = vis_cells.shape[0]
    halves = []
    for index in range(CHUNKS):
        for passed, held in start_chunk(index):
            halves.append((exchange(passed, 0), held))

    row_weights, col_weights = pl.pallas_call(
        weight_kernel,
        out_shape=[
            jax.ShapeDtypeStruct((blocks, SUBW, NVIS), jnp.bfloat16),
            jax.ShapeDtypeStruct((blocks, SUBW, NVIS), jnp.float32),
        ],
        in_specs=[in_smem, in_vmem],
        out_specs=[in_vmem] * 2,
        compiler_params=params,
        cost_estimate=cost(5500000000),
        name="weights",
    )(block_kernel, vis_cells)

    for bit in range(1, bits):
        for index in range(CHUNKS * PARTS):
            passed, held = halved(*halves[index], bit)
            halves[index] = (exchange(passed, bit), held)

    pieces = []
    for index in range(CHUNKS):
        both = halves[index * PARTS : (index + 1) * PARTS]
        parts = {0: jnp.stack([first + second for first, second in both]).astype(jnp.bfloat16)}
        for step in range(1, pairs):
            parts[step] = lax.ppermute(parts[0], "pair", [(p, p ^ step) for p in range(pairs)])
        pieces += [parts[step] for step in range(pairs)]

    return pl.pallas_call(
        functools.partial(degrid_kernel, pairs),
        out_shape=jax.ShapeDtypeStruct((blocks, 2, NVIS), jnp.float32),
        in_specs=[in_smem] * 2 + [in_vmem] * (3 + len(pieces)),
        out_specs=in_vmem,
        scratch_shapes=[pltpu.VMEM((SG_WIDE * SUBW, 2 * SUBW), jnp.bfloat16)],
        compiler_params=params,
        cost_estimate=cost(3300000000),
        name="degrid",
    )(place, block_subgrid, row_weights, col_weights, table_chunked(), *pieces)


def solution(mesh):
    placed = (
        P(("groups", "wide"), None, "pair", None),
        P("groups", None, None),
        P(("groups", "wide", "pair")),
        P(("groups", "wide", "pair"), None),
        P(("groups", "wide", "pair"), None, None),
    )
    return jax.shard_map(
        on_device,
        mesh=mesh,
        in_specs=placed,
        out_specs=P(("groups", "wide", "pair"), None, None),
        check_vma=False,
    )
```
